32 devices in a mesh: tm: 8 (over y, x, core), space: 4 (over z).
Axes of the slice: x: 2, y: 2, z: 4, core: 2. Of those that a mesh axis runs over, the one named last changes fastest.
Arguments:
- initial_starts: float32 [8, 1024, 512], P('tm', None, 'space'), may hold values from -6 to 6
- source: float32 [8, 1024, 512], P('tm', None, 'space'), may hold values from -12 to 12
- region: int32 [1024, 512], P(None, 'space'), may hold values from 0 to 7
- base_reluctivity: float32 [8], replicated, may hold values from 0.4 to 1
- saturation: float32 [8], replicated, may hold values from 0.2 to 1
- mobility: float32 [8], replicated, may hold values from 0.01 to 0.12
Outputs:
- final_starts: float32 [8, 1024, 512], P('tm', None, 'space')
- fine_ends: float32 [8, 1024, 512], P('tm', None, 'space')
The draws below stay inside these ranges and needn't reach their ends.
All inputs are finite; a program needn't handle non-finite values.
Results may differ from the reference program's by a relative error of at most 0.00002.
Values sent between devices are 32-bit elements; how exact they have to be, the bound alone decides.
No kernel may reach another device: no remote copies, remote signals or barrier semaphores. Data moves between devices by JAX's collectives and lax.ppermute only.
A program may use at most 64 MiB of HBM per device.

```python
import math
import jax
import jax.numpy as jnp
from jax import lax

RADIAL = 1024
REGIONS = 8
STEPS = 3
ITERS = 2
SLICES = 8
ANGLES = 512


def with_ends(values, stream_key, smallest, top_value):
    longest = values.shape.index(max(values.shape))
    spots = []
    for shift in (0, 1):
        where = [jax.random.randint(jax.random.fold_in(stream_key, axis), (), 0, length) for axis, length in enumerate(values.shape)]
        where[longest] = (where[longest] + shift) % values.shape[longest]
        spots.append(tuple(where))
    return values.at[spots[0]].set(smallest).at[spots[1]].set(top_value)


def shard_levels(stream_key, extent, split, low, largest):
    loudness, own = 1.0, jax.random.fold_in(stream_key, 6)
    for dim, shards_of in split:
        draws = jnp.exp(jax.random.uniform(jax.random.fold_in(own, dim), (shards_of,), jnp.float32, low / len(split), largest / len(split)))
        loudness = loudness * jnp.repeat(draws, extent[dim] // shards_of).reshape([-1 if axis == dim else 1 for axis in range(len(extent))])
    return loudness


def normal_values(stream_key, shape, width, bound, shards=(), kind=jnp.bfloat16):
    gain = shard_levels(stream_key, shape, shards, -0.22, 0.18) if shards else 1.0
    drawn = jax.random.normal(stream_key, shape, jnp.float32) * width * gain
    return jnp.minimum(jnp.maximum(drawn, -bound), bound).astype(kind)


def setup_inputs(seed: int = 0) -> dict:
    streams_of = jax.random.split(jax.random.key(seed), 7)
    initial_starts = normal_values(streams_of[0], (SLICES, RADIAL, ANGLES), 1.0, 6.0, ((0, 8), (2, 4)), jnp.float32)
    source = normal_values(streams_of[1], (SLICES, RADIAL, ANGLES), 2.0, 12.0, ((0, 8), (2, 4)), jnp.float32)
    region = with_ends(jax.random.randint(streams_of[2], (RADIAL, ANGLES), 0, REGIONS), jax.random.fold_in(streams_of[2], 1), 0, REGIONS - 1).astype(jnp.int32)
    base_reluctivity = jnp.clip(jax.random.uniform(streams_of[3], (REGIONS,), jnp.float32, 0.4, 1.0), 0.4, 1.0)
    saturation = jnp.clip(jax.random.uniform(streams_of[4], (REGIONS,), jnp.float32, 0.2, 1.0), 0.2, 1.0)
    mobility = jnp.clip(jnp.exp(jax.random.uniform(streams_of[5], (REGIONS,), jnp.float32, math.log(0.01), math.log(0.12))), 0.01, 0.12)
    return {"initial_starts": initial_starts, "source": source, "region": region, "base_reluctivity": base_reluctivity, "saturation": saturation, "mobility": mobility}


def lookup(region, region_table):
    region_ids = jnp.arange(region_table.shape[0], dtype=jnp.int32)
    picked = jnp.where(region[None] == region_ids[:, None, None], region_table[:, None, None], jnp.float32(0.0))
    return jnp.sum(picked, axis=0)


def wrap_columns(values, margin):
    total = values.shape[1]
    return jnp.concatenate([values[:, total - margin:], values, values[:, :margin]], axis=1)


def advance(potential, base_nu, satur_rate, mobile, driver):
    padded = jnp.pad(potential, ((1, 1), (0, 0)))
    radial_b = (padded[2:, 1:-1] - padded[:-2, 1:-1]) * 0.5
    angle_b = (potential[:, 2:] - potential[:, :-2]) * 0.5
    flux_sq = radial_b * radial_b + angle_b * angle_b
    reluct = base_nu * (1.0 + satur_rate * flux_sq / (1.0 + flux_sq))
    reluct_pad = jnp.pad(reluct, ((1, 1), (0, 0)), mode="edge")
    reluct_mid = reluct[:, 1:-1]
    centre = potential[:, 2:-2]
    east_flux = 0.5 * (reluct_mid + reluct[:, 2:]) * (potential[:, 3:-1] - centre)
    west_flux = 0.5 * (reluct_mid + reluct[:, :-2]) * (potential[:, 1:-3] - centre)
    north_flux = 0.5 * (reluct_mid + reluct_pad[2:, 1:-1]) * (padded[2:, 2:-2] - centre)
    south_flux = 0.5 * (reluct_mid + reluct_pad[:-2, 1:-1]) * (padded[:-2, 2:-2] - centre)
    return centre + mobile * (east_flux + west_flux + north_flux + south_flux + driver)


def reference(initial_starts, source, region, base_reluctivity, saturation, mobility):
    base_nu = lookup(region, base_reluctivity)
    satur_rate = lookup(region, saturation)
    mobile = lookup(region, mobility)
    coarse_gain = 1.0 / (1.0 + 12.0 * mobile * base_nu)
    base_wide = wrap_columns(base_nu, 1)
    satur_wide = wrap_columns(satur_rate, 1)

    def run_slice(slice_pair):
        potential = slice_pair[0]
        for segment in range(STEPS):
            potential = advance(wrap_columns(potential, 2), base_wide, satur_wide, mobile, slice_pair[1])
        return potential

    starts = initial_starts
    fine_ends = initial_starts
    for iteration in range(ITERS):
        fine_ends = lax.map(run_slice, (starts, source))
        corrected = fine_ends - coarse_gain[None] * starts
        previous = fine_ends[SLICES - 1]
        collected = [previous]
        for slot in range(1, SLICES):
            previous = coarse_gain * previous + corrected[slot - 1]
            collected.append(previous)
        starts = jnp.stack(collected)
    return starts, fine_ends
```

```python
import functools

import jax
import jax.numpy as jnp
import numpy as np
from jax import lax
from jax.experimental import pallas as pl
from jax.experimental.pallas import tpu as pltpu
from jax.sharding import PartitionSpec as P

STEPS = 3
ITERS = 2
HALO = 2 * STEPS * ITERS
REACH = 2 * STEPS
PAD = 8
CHUNK = 48
FOLD = 8
VMEM = pl.BlockSpec(memory_space=pltpu.VMEM)
SMEM = pl.BlockSpec(memory_space=pltpu.SMEM)
PARAMS = pltpu.CompilerParams(vmem_limit_bytes=24 * 1024 * 1024)


def lanes_of(rows, lanes):
    return lax.broadcasted_iota(jnp.int32, (rows, lanes), 1)


def roll(x, amount):
    return pltpu.roll(x, amount % x.shape[1], 1)


def inside(lane, *spans):
    hit = None
    for low, high in spans:
        one = (lane >= low) & (lane < high)
        hit = one if hit is None else hit | one
    return hit


def over_chunks(rows, body):
    chunk = max(n for n in range(8, CHUNK + 1, 8) if rows % n == 0)

    def step(c, carry):
        body(pl.multiple_of(c * chunk, 8), chunk)
        return carry

    lax.fori_loop(0, rows // chunk, step, 0)


def coefficients(region, nu_tab, sat_tab, mob_tab):
    base = jnp.zeros(region.shape, jnp.float32)
    satur, mobile = base, base
    for r in range(nu_tab.shape[0]):
        hit = region == r
        base = jnp.where(hit, nu_tab[r], base)
        satur = jnp.where(hit, sat_tab[r], satur)
        mobile = jnp.where(hit, mob_tab[r], mobile)
    gain = 1.0 / (1.0 + 12.0 * mobile * base)
    slope = base * satur
    return base + slope, slope, mobile * 0.5, gain


def fine_steps(units, rows):
    for bufs, nu, top, slope, mob, drive in units:
        for old, new in zip(bufs[:-1], bufs[1:]):

            def first(base, n, old=old, nu=nu, top=top, slope=slope):
                here = old[pl.ds(base + PAD, n), :]
                dr = old[pl.ds(base + PAD + 1, n), :] - old[pl.ds(base + PAD - 1, n), :]
                dt = roll(here, -1) - roll(here, 1)
                bottom = 1.0 + 0.25 * (dr * dr + dt * dt)
                nu[pl.ds(base + PAD, n), :] = top[pl.ds(base, n), :] - slope[pl.ds(base, n), :] / bottom

            over_chunks(rows, first)
            nu[PAD - 1 : PAD, :] = nu[PAD : PAD + 1, :]
            nu[PAD + rows : PAD + rows + 1, :] = nu[PAD + rows - 1 : PAD + rows, :]

            def second(base, n, old=old, new=new, nu=nu, mob=mob, drive=drive):
                here = old[pl.ds(base + PAD, n), :]
                nu0 = nu[pl.ds(base + PAD, n), :]
                east = (nu0 + roll(nu0, -1)) * (roll(here, -1) - here)
                total = east - roll(east, 1)
                north = (nu0 + nu[pl.ds(base + PAD + 1, n), :]) * (old[pl.ds(base + PAD + 1, n), :] - here)
                south = (nu0 + nu[pl.ds(base + PAD - 1, n), :]) * (old[pl.ds(base + PAD - 1, n), :] - here)
                total = total + north + south + drive[pl.ds(base, n), :]
                new[pl.ds(base + PAD, n), :] = here + mob[pl.ds(base, n), :] * total

            over_chunks(rows, second)


def clear_pads(ref, rows):
    ref[0:PAD, :] = jnp.zeros((PAD, ref.shape[1]), jnp.float32)
    ref[PAD + rows : rows + 2 * PAD, :] = jnp.zeros((PAD, ref.shape[1]), jnp.float32)


def pack_kernel(rows, start, core, own_a, own_j, got, region, a0, a1, j0, j1, to_west, to_east):
    h = core[0]
    q = a0.shape[1] // 4
    clear_pads(a0, rows)
    clear_pads(a1, rows)
    first = h * start

    def body(base, n):
        lane = lanes_of(n, a0.shape[1])
        src = pl.ds(pl.multiple_of(first + base, 8), n)
        a_own, j_own = own_a[src, :], own_j[src, :]
        a_got = got[pl.ds(base, n), :]
        j_got = got[pl.ds(pl.multiple_of(base + rows, 8), n), :]
        mine = h == 0
        a_0, a_1 = jnp.where(mine, a_own, a_got), jnp.where(mine, a_got, a_own)
        j_0, j_1 = jnp.where(mine, j_own, j_got), jnp.where(mine, j_got, j_own)
        a0[pl.ds(base + PAD, n), :] = a_0
        a1[pl.ds(base + PAD, n), :] = a_1
        j0[pl.ds(base, n), :] = j_0 * 2.0
        j1[pl.ds(base, n), :] = j_1 * 2.0
        ids = region[src, :].astype(jnp.float32)
        out = jnp.zeros((n, a0.shape[1]), jnp.float32)
        for part, (first0, second0) in enumerate(((a_0, a_1), (j_0, j_1), (ids, ids))):
            for s, x in enumerate((first0, second0)):
                at = (2 * s + 2) * q - HALO * (part + 1)
                out = jnp.where(inside(lane, (at, at + HALO)), roll(x, at), out)
        to_west[pl.ds(base, n), :] = out
        out = jnp.zeros((n, a0.shape[1]), jnp.float32)
        for part, (first0, second0) in enumerate(((a_0, a_1), (j_0, j_1), (ids, ids))):
            for s, x in enumerate((first0, second0)):
                at = 2 * s * q + HALO * part
                out = jnp.where(inside(lane, (at, at + HALO)), roll(x, at + HALO), out)
        to_east[pl.ds(base, n), :] = out

    over_chunks(rows, body)


def own_part(s0, s1, lane, rest):
    q = s0.shape[1] // 4
    out = rest
    for s, x in enumerate((s0, s1)):
        w = 2 * s * q
        out = jnp.where(inside(lane, (w + HALO, w + q)), roll(x, w + HALO), out)
        out = jnp.where(inside(lane, (w + q, w + 2 * q - HALO)), roll(x, w + 2 * q - HALO), out)
    return out


def merge_edges(main, strip, s, lane):
    lanes = main.shape[1]
    q = lanes // 4
    w = 2 * s * q
    out = jnp.where(lane < REACH, roll(strip, -(w + HALO)), main)
    return jnp.where(lane >= lanes - REACH, roll(strip, -(w + 2 * q - HALO)), out)


def main_kernel(rows, start, core, nu_tab, sat_tab, mob_tab, region, a0, a1, j0, j1, f0, f1, top, slope, mob, gain, b, c, nu):
    first = core[0] * start
    for ref in (b, c):
        clear_pads(ref, rows)

    def body(base, n):
        ids = region[pl.ds(pl.multiple_of(first + base, 8), n), :]
        here = pl.ds(base, n)
        top[here, :], slope[here, :], mob[here, :], gain[here, :] = coefficients(ids, nu_tab, sat_tab, mob_tab)

    over_chunks(rows, body)
    fine_steps(
        (((a0, b, c, f0), nu, top, slope, mob, j0), ((a1, b, c, f1), nu, top, slope, mob, j1)), rows
    )


def strip_kernel(
    rows, cut, flags, nu_tab, sat_tab, mob_tab, west, east, region, a0, a1, j0, j1, f0, f1, gain,
    top_s, slope_s, mob_s, gain_s, j_s, corr, corr_s, d_a, d_b, g_a, g_b, a_s, b_s, c_s, nu, d_s,
):
    lanes = a0.shape[1]
    q = lanes // 4
    first = flags[0] * flags[2]
    last = flags[1] == 1
    for ref in (a_s, b_s, c_s):
        clear_pads(ref, rows)

    def build(base, n):
        lane = lanes_of(n, lanes)
        here, padded = pl.ds(base, n), pl.ds(base + PAD, n)
        w, e = west[here, :], east[here, :]
        heads = inside(lane, (0, HALO), (2 * q, 2 * q + HALO))
        a_s[padded, :] = own_part(a0[padded, :], a1[padded, :], lane, jnp.where(heads, w, e))
        rest = jnp.where(heads, roll(w, -HALO), roll(e, HALO)) * 2.0
        j_s[here, :] = own_part(j0[here, :], j1[here, :], lane, rest)
        ids = region[pl.ds(pl.multiple_of(first + base, 8), n), :].astype(jnp.float32)
        rest = jnp.where(heads, roll(w, -2 * HALO), roll(e, 2 * HALO))
        ids = own_part(ids, ids, lane, rest).astype(jnp.int32)
        top_s[here, :], slope_s[here, :], mob_s[here, :], gain_s[here, :] = coefficients(
            ids, nu_tab, sat_tab, mob_tab
        )

    over_chunks(rows, build)
    fine_steps((((a_s, b_s, c_s, b_s), nu, top_s, slope_s, mob_s, j_s),), rows)

    def finish(base, n):
        lane = lanes_of(n, lanes)
        here, padded = pl.ds(base, n), pl.ds(base + PAD, n)
        strip = b_s[padded, :]
        g_s = gain_s[here, :]
        c = strip - g_s * a_s[padded, :]
        corr_s[here, :] = c
        d_s[here, :] = jnp.where(last, roll(strip, 2 * q), g_s * c + roll(c, 2 * q))
        g = gain[here, :]
        end0 = merge_edges(f0[padded, :], strip, 0, lane)
        end1 = merge_edges(f1[padded, :], strip, 1, lane)
        c0 = end0 - g * a0[padded, :]
        corr[here, :] = c0
        nu[here, :] = jnp.where(last, end1, g * c0 + end1 - g * a1[padded, :])

    over_chunks(rows, finish)
    d_a[...] = nu[0:cut, :]
    g_a[...] = gain[0:cut, :]
    d_b[0 : rows - cut, :] = nu[cut:rows, :]
    g_b[0 : rows - cut, :] = gain[cut:rows, :]
    fold(d_s, d_b, rows, rows - cut)
    fold(gain_s, g_b, rows, rows - cut)


def fold_tiles(rows):
    return -(-(rows // 8) // FOLD)


def fold(src, dst, rows, at):
    lanes = src.shape[1]
    q, width = lanes // 4, lanes // FOLD
    lane = lanes_of(8, lanes)
    tiles = fold_tiles(rows)
    for r in range(tiles):
        out = jnp.zeros((8, lanes), jnp.float32)
        for k in range(FOLD):
            t = k * tiles + r
            if 8 * t >= rows:
                continue
            x = src[8 * t : 8 * t + 8, :]
            at_w, at_e = width * k, width * k + width // 2
            out = jnp.where(inside(lane, (at_w, at_w + REACH)), roll(x, at_w - (HALO - REACH)), out)
            out = jnp.where(inside(lane, (at_e, at_e + REACH)), roll(x, at_e - (2 * q - HALO)), out)
        dst[at + 8 * r : at + 8 * r + 8, :] = out


def unfold(src, at, dst, rows):
    lanes = src.shape[1]
    q, width = lanes // 4, lanes // FOLD
    lane = lanes_of(8, lanes)
    tiles = fold_tiles(rows)
    for r in range(tiles):
        x = src[at + 8 * r : at + 8 * r + 8, :]
        for k in range(FOLD):
            t = k * tiles + r
            if 8 * t >= rows:
                continue
            at_w, at_e = width * k, width * k + width // 2
            out = jnp.where(lane < q, roll(x, HALO - REACH - at_w), roll(x, 2 * q - HALO - at_e))
            dst[8 * t : 8 * t + 8, :] = out


def second_kernel(
    rows, half, cut, flags, s_a, s_b, corr, corr_s, gain, top, slope, mob, j0, j1,
    gain_s, top_s, slope_s, mob_s, j_s,
    end_own, end_send, d_out, corr_out, gain_out, a0, a1, a_s, b0, b1, b_s, c, nu, spread,
):
    lanes = a0.shape[1]
    q = lanes // 4
    h = flags[0]
    last = flags[1] == 1
    for ref in (a0, a1, a_s, b0, b1, b_s, c):
        clear_pads(ref, rows)
    a0[PAD : PAD + cut, :] = s_a[...]
    a0[PAD + cut : PAD + rows, :] = s_b[0 : rows - cut, :]
    unfold(s_b, rows - cut, spread, rows)

    def build(base, n):
        lane = lanes_of(n, lanes)
        here, padded = pl.ds(base, n), pl.ds(base + PAD, n)
        s = a0[padded, :]
        a1[padded, :] = gain[here, :] * s + corr[here, :]
        strip = spread[here, :]
        strip = jnp.where(inside(lane, (HALO, q)), roll(s, HALO), strip)
        strip = jnp.where(inside(lane, (q, 2 * q - HALO)), roll(s, 2 * q - HALO), strip)
        other = roll(gain_s[here, :] * strip + corr_s[here, :], 2 * q)
        a_s[padded, :] = jnp.where(lane < 2 * q, strip, other)

    over_chunks(rows, build)
    fine_steps(
        (
            ((a0, b0, c, b0), nu, top, slope, mob, j0),
            ((a1, b1, c, b1), nu, top, slope, mob, j1),
            ((a_s, b_s, c, b_s), nu, top_s, slope_s, mob_s, j_s),
        ),
        rows,
    )

    def finish(base, n):
        lane = lanes_of(n, lanes)
        here = pl.ds(base, n)
        at = pl.multiple_of(base + h * (rows - half), 8)
        inner, padded = pl.ds(at, n), pl.ds(at + PAD, n)
        strip = b_s[padded, :]
        end0 = merge_edges(b0[padded, :], strip, 0, lane)
        end1 = merge_edges(b1[padded, :], strip, 1, lane)
        end_own[here, :] = jnp.where(h == 0, end0, end1)
        end_send[here, :] = jnp.where(h == 0, end1, end0)
        g = gain[inner, :]
        c0 = end0 - g * a0[padded, :]
        corr_out[here, :] = c0
        gain_out[here, :] = g
        d_out[here, :] = jnp.where(last, end1, g * c0 + end1 - g * a1[padded, :])

    over_chunks(half, finish)


def last_kernel(flags, s, corr, gain, own, send):
    h = flags[0]

    def body(base, n):
        here = pl.ds(base, n)
        new0 = s[here, :]
        new1 = gain[here, :] * new0 + corr[here, :]
        own[here, :] = jnp.where(h == 0, new0, new1)
        send[here, :] = jnp.where(h == 0, new1, new0)

    over_chunks(s.shape[0], body)


def join_kernel(half, flags, own, got, out):
    h = flags[0]
    out[pl.ds(pl.multiple_of(h * half, 8), half), :] = own[...]
    out[pl.ds(pl.multiple_of((1 - h) * half, 8), half), :] = got[...]


def call(kernel, outs, scratch=(), smem=1, cost=None):
    def run(*operands):
        return pl.pallas_call(
            kernel,
            out_shape=[jax.ShapeDtypeStruct(shape, jnp.float32) for shape in outs],
            in_specs=[SMEM] * smem + [VMEM] * (len(operands) - smem),
            out_specs=[VMEM] * len(outs),
            scratch_shapes=[pltpu.VMEM(shape, jnp.float32) for shape in scratch],
            compiler_params=PARAMS,
            cost_estimate=cost,
        )(*operands)

    return run


def scan_plan(chips):
    levels = chips.bit_length() - 1
    every = range(chips)
    end = chips - 1
    own = [end if c == end else -1 for c in every]
    rising = []
    for b in range(levels):
        size = 1 << b
        into, keep, came = [], [], []
        for c in every:
            closes = (c >> (b + 1)) == (end >> (b + 1))
            if c & size:
                into.append(c % size)
                keep.append(0)
                came.append(-1 if closes else size)
            else:
                into.append(c if closes else -1)
                keep.append(-1 if closes else size)
                came.append(0)
        rising.append((b, into, keep, came))
    if levels != 2:
        return own, (rising, rising)

    def weight(to, at):
        return max(to - (at + 1) % chips, -1)

    turned = [
        (1, [weight(c, c ^ 2) for c in every], [weight(c ^ 1, c) for c in every], [weight(c ^ 1, c ^ 2) for c in every]),
        (0, [0 for c in every], None, None),
    ]
    return own, (rising, turned)


def power(square, exponents, chip):
    most = max(exponents)
    e = jnp.asarray(np.array(exponents, np.int32))[chip]
    value, factor = jnp.ones_like(square), square
    for k in range(max(most, 0).bit_length()):
        value = jnp.where((e >> k) & 1 == 1, value * factor, value)
        factor = factor * factor
    return jnp.where(e < 0, jnp.float32(0.0), value)


def scan(parts, gains, chip, chips, count):
    own, orders = scan_plan(chips)
    squares = [g * g for g in gains]
    sums = [power(sq, own, chip) * d for sq, d in zip(squares, parts)]
    passed = list(parts)
    for stage in range(len(orders[0])):
        arrived = []
        for p, order in enumerate(orders):
            pairs = [(i, i ^ (2 << order[stage][0])) for i in range(count)]
            arrived.append(lax.ppermute(passed[p], "tm", pairs))
        for p, order in enumerate(orders):
            _, into, keep, came = order[stage]
            sums[p] = sums[p] + power(squares[p], into, chip) * arrived[p]
            if stage + 1 < len(order):
                passed[p] = (
                    power(squares[p], keep, chip) * passed[p] + power(squares[p], came, chip) * arrived[p]
                )
    return sums


def local(initial_starts, source, region, base_reluctivity, saturation, mobility):
    potential, driver = initial_starts[0], source[0]
    radial, lanes = potential.shape
    count = lax.axis_size("tm")
    chips = count // 2
    spaces = lax.axis_size("space")
    slot = lax.axis_index("tm")
    h, chip = slot % 2, slot // 2
    half = radial // 2
    margin = -(-HALO // 8) * 8
    rows, start = half + margin, half - margin
    flags = jnp.stack([h, (chip == chips - 1).astype(jnp.int32), jnp.int32(start)]).astype(jnp.int32)
    tables = (base_reluctivity, saturation, mobility)
    partner = [(i, i ^ 1) for i in range(count)]
    slab, padded = (rows, lanes), (rows + 2 * PAD, lanes)
    cost = pl.CostEstimate(flops=240 * rows * lanes, bytes_accessed=40 * rows * lanes, transcendentals=0)

    there = (1 - h) * start
    send = jnp.concatenate(
        [lax.dynamic_slice(x, (there, 0), slab) for x in (potential, driver)], axis=0
    )
    got = lax.ppermute(send, "tm", partner)
    a0, a1, j0, j1, to_west, to_east = call(
        functools.partial(pack_kernel, rows, start), (padded, padded, slab, slab, slab, slab), cost=cost
    )(flags, potential, driver, got, region)
    from_east = lax.ppermute(to_west, "space", [((i + 1) % spaces, i) for i in range(spaces)])
    from_west = lax.ppermute(to_east, "space", [(i, (i + 1) % spaces) for i in range(spaces)])
    f0, f1, top, slope, mob, gain = call(
        functools.partial(main_kernel, rows, start),
        (padded, padded, slab, slab, slab, slab), (padded, padded, padded), smem=4, cost=cost,
    )(flags, *tables, region, a0, a1, j0, j1)

    tail = 8 * fold_tiles(rows)
    cut = 8 * (-(-(rows + tail) // 16))
    part_a, part_b = (cut, lanes), (rows - cut + tail, lanes)
    top_s, slope_s, mob_s, gain_s, j_s, corr, corr_s, d_a, d_b, g_a, g_b = call(
        functools.partial(strip_kernel, rows, cut),
        (slab, slab, slab, slab, slab, slab, slab, part_a, part_b, part_a, part_b),
        (padded, padded, padded, padded, slab), smem=4, cost=cost,
    )(flags, *tables, from_west, from_east, region, a0, a1, j0, j1, f0, f1, gain)
    s_a, s_b = scan((d_a, d_b), (g_a, g_b), chip, chips, count)

    own_rows = (half, lanes)
    end_own, end_send, d_out, corr_2, gain_2 = call(
        functools.partial(second_kernel, rows, half, cut),
        (own_rows, own_rows, own_rows, own_rows, own_rows),
        (padded, padded, padded, padded, padded, padded, padded, padded, slab), cost=cost,
    )(flags, s_a, s_b, corr, corr_s, gain, top, slope, mob, j0, j1, gain_s, top_s, slope_s, mob_s, j_s)
    quarter = half // 2
    s_2 = scan(
        (d_out[:quarter], d_out[quarter:]), (gain_2[:quarter], gain_2[quarter:]), chip, chips, count
    )
    end_got = lax.ppermute(end_send, "tm", partner)
    (ends,) = call(functools.partial(join_kernel, half), ((radial, lanes),))(flags, end_own, end_got)
    new_own, new_send = call(last_kernel, (own_rows, own_rows))(
        flags, jnp.concatenate(s_2, axis=0), corr_2, gain_2
    )
    new_got = lax.ppermute(new_send, "tm", partner)
    (starts,) = call(functools.partial(join_kernel, half), ((radial, lanes),))(flags, new_own, new_got)
    return (starts[None], ends[None])


def solution(mesh):
    placed = (P("tm", None, "space"), P("tm", None, "space"), P(None, "space"), P(), P(), P())
    return jax.shard_map(
        local,
        mesh=mesh,
        in_specs=placed,
        out_specs=(P("tm", None, "space"), P("tm", None, "space")),
        check_vma=False,
    )
```

```python
import functools

import jax
import jax.numpy as jnp
import numpy as np
from jax import lax
from jax.experimental import pallas as pl
from jax.experimental.pallas import tpu as pltpu
from jax.sharding import PartitionSpec as P

STEPS = 3
ITERS = 2
HALO = 2 * STEPS * ITERS
J_HALO = HALO - 2
ID_HALO = HALO - 1
REACH = 2 * STEPS
PAD = 8
CHUNK = 88
FOLD = 8
VMEM = pl.BlockSpec(memory_space=pltpu.VMEM)
FLAGS = 3
SMEM = pl.BlockSpec(memory_space=pltpu.SMEM)
PARAMS = pltpu.CompilerParams(vmem_limit_bytes=14 * 1024 * 1024)


def lanes_of(rows, lanes):
    return lax.broadcasted_iota(jnp.int32, (rows, lanes), 1)


def roll(x, amount):
    amount = amount % x.shape[1]
    return pltpu.roll(x, amount, 1) if amount else x


def inside(lane, *spans):
    hit = None
    for low, high in spans:
        one = (lane >= low) & (lane < high)
        hit = one if hit is None else hit | one
    return hit


def over_chunks(rows, body):
    chunk = max(n for n in range(8, CHUNK + 1, 8) if rows % n == 0)
    for base in range(0, rows, chunk):
        body(base, chunk)


def aligned(at):
    return at if isinstance(at, int) else pl.multiple_of(at, 8)


def coefficients(region, nu_tab, sat_tab, mob_tab):
    base = jnp.zeros(region.shape, jnp.float32)
    satur, mobile = base, base
    for r in range(nu_tab.shape[0]):
        hit = region == r
        base = jnp.where(hit, nu_tab[r], base)
        satur = jnp.where(hit, sat_tab[r], satur)
        mobile = jnp.where(hit, mob_tab[r], mobile)
    gain = 1.0 / (1.0 + 12.0 * mobile * base)
    slope = base * satur
    return base + slope, slope, mobile * 0.5, gain


def fine_steps(units, rows, work):
    chunk = max(n for n in range(8, CHUNK + 1, 8) if rows % n == 0)
    chunks = rows // chunk
    for step in range(STEPS):
        moved = {}
        for turn in range(chunks + 4):
            for u, (bufs, top, slope, mob, drive) in enumerate(units):
                old, new = bufs[step], bufs[step + 1]
                nu, east, flow, face = work[4 * u : 4 * u + 4]
                c = turn - 3
                if 0 <= c < chunks:
                    at = c * chunk + PAD
                    nu0 = nu[pl.ds(at, chunk), :]
                    out = (nu0 + moved.pop((u, 3, c))) * east[pl.ds(at, chunk), :]
                    flow[pl.ds(at, chunk), :] = out
                    moved[u, 4, c] = roll(out, 1)
                    face[pl.ds(at, chunk), :] = (nu0 + nu[pl.ds(at - 1, chunk), :]) * (
                        old[pl.ds(at, chunk), :] - old[pl.ds(at - 1, chunk), :]
                    )
                    if c == chunks - 1:
                        at = PAD + rows
                        nu[at : at + 1, :] = nu[at - 1 : at, :]
                        face[pl.ds(at, 8), :] = (nu[pl.ds(at, 8), :] + nu[pl.ds(at - 1, 8), :]) * (
                            old[pl.ds(at, 8), :] - old[pl.ds(at - 1, 8), :]
                        )
                c = turn - 4
                if 0 <= c < chunks:
                    at, here_rows = c * chunk + PAD, pl.ds(c * chunk, chunk)
                    total = flow[pl.ds(at, chunk), :] - moved.pop((u, 4, c))
                    total = total + (face[pl.ds(at + 1, chunk), :] - face[pl.ds(at, chunk), :])
                    total = total + drive[here_rows, :]
                    new[pl.ds(at, chunk), :] = old[pl.ds(at, chunk), :] + mob[here_rows, :] * total
                c = turn - 2
                if 0 <= c < chunks:
                    at, here_rows = c * chunk + PAD, pl.ds(c * chunk, chunk)
                    dr = old[pl.ds(at + 1, chunk), :] - old[pl.ds(at - 1, chunk), :]
                    dt = east[pl.ds(at, chunk), :] + moved.pop((u, 2, c))
                    bottom = 1.0 + (dr * dr + dt * dt)
                    out = top[here_rows, :] - slope[here_rows, :] / bottom
                    nu[pl.ds(at, chunk), :] = out
                    if c == 0:
                        nu[PAD - 1 : PAD, :] = nu[PAD : PAD + 1, :]
                    moved[u, 3, c] = roll(out, -1)
                c = turn - 1
                if 0 <= c < chunks:
                    at = c * chunk + PAD
                    out = moved.pop((u, 1, c)) - old[pl.ds(at, chunk), :]
                    east[pl.ds(at, chunk), :] = out
                    moved[u, 2, c] = roll(out, 1)
                c = turn
                if 0 <= c < chunks:
                    moved[u, 1, c] = roll(old[pl.ds(c * chunk + PAD, chunk), :], -1)


def clear_pads(ref, rows):
    ref[0:PAD, :] = jnp.zeros((PAD, ref.shape[1]), jnp.float32)
    ref[PAD + rows : rows + 2 * PAD, :] = jnp.zeros((PAD, ref.shape[1]), jnp.float32)


def pack_kernel(rows, start, flags, own_a, own_j, got, region, a0, a1, j0, j1, to_west, to_east):
    lanes = a0.shape[1]
    q, both, tall = lanes // 4, HALO + J_HALO, rows // 2
    mine = flags[0] == 0
    first = flags[0] * start
    clear_pads(a0, rows)
    clear_pads(a1, rows)

    def body(low, n):
        lane = lanes_of(n, lanes)
        west = jnp.zeros((n, lanes), jnp.float32)
        east = west
        for k in range(2):
            base = low + k * tall
            src = pl.ds(aligned(first + base), n)
            a_own, j_own = own_a[src, :], own_j[src, :]
            a_got, j_got = got[pl.ds(base, n), :], got[pl.ds(base + rows, n), :]
            a_0, a_1 = jnp.where(mine, a_own, a_got) * 0.5, jnp.where(mine, a_got, a_own) * 0.5
            j_0, j_1 = jnp.where(mine, j_own, j_got), jnp.where(mine, j_got, j_own)
            a0[pl.ds(base + PAD, n), :] = a_0
            a1[pl.ds(base + PAD, n), :] = a_1
            j0[pl.ds(base, n), :] = j_0
            j1[pl.ds(base, n), :] = j_1
            ids = region[src, :].astype(jnp.float32)
            for s, (a, j) in enumerate(((a_0, j_0), (a_1, j_1))):
                at = (2 * s + 2) * q - HALO - k * both
                west = jnp.where(inside(lane, (at, at + HALO)), roll(a, at), west)
                at = at - J_HALO
                west = jnp.where(inside(lane, (at, at + J_HALO)), roll(j, at), west)
                at = 2 * s * q + k * both
                east = jnp.where(inside(lane, (at, at + HALO)), roll(a, at + HALO), east)
                at = at + HALO
                east = jnp.where(inside(lane, (at, at + J_HALO)), roll(j, at + J_HALO), east)
            at = 2 * q * (1 - k)
            west = jnp.where(inside(lane, (at, at + ID_HALO)), roll(ids, at), west)
            at = (3 - 2 * k) * q + HALO
            east = jnp.where(inside(lane, (at, at + ID_HALO)), roll(ids, at + ID_HALO), east)
        to_west[pl.ds(low, n), :] = west
        to_east[pl.ds(low, n), :] = east

    over_chunks(tall, body)


def own_part(s0, s1, lane):
    q = s0.shape[1] // 4
    out = jnp.zeros(s0.shape, jnp.float32)
    for s, x in enumerate((s0, s1)):
        w = 2 * s * q
        out = jnp.where(inside(lane, (w + HALO, w + q)), roll(x, w + HALO), out)
        out = jnp.where(inside(lane, (w + q, w + 2 * q - HALO)), roll(x, w + 2 * q - HALO), out)
    return out


def merge_edges(main, strip, s, lane):
    lanes = main.shape[1]
    q = lanes // 4
    w = 2 * s * q
    out = jnp.where(lane < REACH, roll(strip, -(w + HALO)), main)
    return jnp.where(lane >= lanes - REACH, roll(strip, -(w + 2 * q - HALO)), out)


def main_kernel(
    rows, start, flags, nu_tab, sat_tab, mob_tab, region, a0, a1, j0, j1,
    f0, f1, top, slope, mob, gain, a_own, j_own, id_own, b0, c0, b1, c1, *work,
):
    first = flags[0] * start
    for ref in (b0, c0, b1, c1):
        clear_pads(ref, rows)

    def body(base, n):
        lane = lanes_of(n, a0.shape[1])
        ids = region[pl.ds(aligned(first + base), n), :]
        here, padded = pl.ds(base, n), pl.ds(base + PAD, n)
        top[here, :], slope[here, :], mob[here, :], gain[here, :] = coefficients(ids, nu_tab, sat_tab, mob_tab)
        a_own[here, :] = own_part(a0[padded, :], a1[padded, :], lane)
        j_own[here, :] = own_part(j0[here, :], j1[here, :], lane)
        ids = ids.astype(jnp.float32)
        id_own[here, :] = own_part(ids, ids, lane)

    over_chunks(rows, body)
    fine_steps((((a0, b0, c0, f0), top, slope, mob, j0), ((a1, b1, c1, f1), top, slope, mob, j1)), rows, work)


def strip_kernel(
    rows, cut, tail_cut, flags, nu_tab, sat_tab, mob_tab, west, east, a_own, j_own, id_own,
    a0, a1, f0, f1, gain,
    top_s, slope_s, mob_s, gain_s, j_s, corr, corr_s, d_a, d_b, g_a, g_b, a_s, b_s, c_s, d_s, folded, *work,
):
    lanes = a0.shape[1]
    q, both, tall = lanes // 4, HALO + J_HALO, rows // 2
    last = flags[1] == 1
    for ref in (a_s, b_s, c_s):
        clear_pads(ref, rows)

    def build(low, n):
        lane = lanes_of(n, lanes)
        heads = inside(lane, (0, HALO), (2 * q, 2 * q + HALO))
        tails = inside(lane, (2 * q - HALO, 2 * q), (4 * q - HALO, 4 * q))
        w, e = west[pl.ds(low, n), :], east[pl.ds(low, n), :]
        w_ids = roll(w, 1 - (3 * q + HALO)), roll(w, 1 - (q + HALO))
        e_ids = roll(e, -HALO), roll(e, 2 * q - HALO)
        for k in range(2):
            base = low + k * tall
            here, padded = pl.ds(base, n), pl.ds(base + PAD, n)

            def halo(from_west, from_east, rest):
                return jnp.where(heads, from_west, jnp.where(tails, from_east, rest))

            a_s[padded, :] = halo(roll(w, -both) if k else w, roll(e, both) if k else e, a_own[here, :])
            j_s[here, :] = halo(
                roll(w, -J_HALO - k * both), roll(e, J_HALO + k * both), j_own[here, :]
            )
            lower = lane < 2 * q
            ids = halo(
                jnp.where(lower, w_ids[k], w_ids[1 - k]), jnp.where(lower, e_ids[k], e_ids[1 - k]), id_own[here, :]
            )
            top_s[here, :], slope_s[here, :], mob_s[here, :], gain_s[here, :] = coefficients(
                ids.astype(jnp.int32), nu_tab, sat_tab, mob_tab
            )

    over_chunks(tall, build)
    fine_steps((((a_s, b_s, c_s, b_s), top_s, slope_s, mob_s, j_s),), rows, work)

    def finish(base, n):
        lane = lanes_of(n, lanes)
        here, padded = pl.ds(base, n), pl.ds(base + PAD, n)
        strip = b_s[padded, :]
        g_s = gain_s[here, :]
        c = strip - g_s * a_s[padded, :]
        corr_s[here, :] = c
        d_s[here, :] = roll(jnp.where(last, strip, c), 2 * q) + jnp.where(last, 0.0, g_s * c)
        g = gain[here, :]
        end0 = merge_edges(f0[padded, :], strip, 0, lane)
        end1 = merge_edges(f1[padded, :], strip, 1, lane)
        change = end0 - g * a0[padded, :]
        corr[here, :] = change
        out = jnp.where(last, end1, g * change + end1 - g * a1[padded, :])
        to, g_to, at = (d_a, g_a, base) if base < cut else (d_b, g_b, base - cut)
        to[pl.ds(at, n), :] = out
        g_to[pl.ds(at, n), :] = g

    over_chunks(rows, finish)
    for src, part_a, part_b in ((d_s, d_a, d_b), (gain_s, g_a, g_b)):
        fold(src, folded, rows)
        part_a[cut : cut + tail_cut, :] = folded[0:tail_cut, :]
        part_b[rows - cut : rows - cut + folded.shape[0] - tail_cut, :] = folded[tail_cut:, :]


def fold_tiles(rows):
    return -(-(rows // 8) // FOLD)


def fold(src, dst, rows):
    lanes = src.shape[1]
    q, width = lanes // 4, lanes // FOLD
    lane = lanes_of(8, lanes)
    tiles = fold_tiles(rows)
    for r in range(tiles):
        out = jnp.zeros((8, lanes), jnp.float32)
        for k in range(FOLD):
            t = k * tiles + r
            if 8 * t >= rows:
                continue
            x = src[8 * t : 8 * t + 8, :]
            at_w, at_e = width * k, width * k + width // 2
            out = jnp.where(inside(lane, (at_w, at_w + REACH)), roll(x, at_w - (HALO - REACH)), out)
            out = jnp.where(inside(lane, (at_e, at_e + REACH)), roll(x, at_e - (2 * q - HALO)), out)
        dst[8 * r : 8 * r + 8, :] = out


def unfold(src, dst, rows):
    lanes = src.shape[1]
    q, width = lanes // 4, lanes // FOLD
    lane = lanes_of(8, lanes)
    tiles = fold_tiles(rows)
    for r in range(tiles):
        x = src[8 * r : 8 * r + 8, :]
        for k in range(FOLD):
            t = k * tiles + r
            if 8 * t >= rows:
                continue
            at_w, at_e = width * k, width * k + width // 2
            out = jnp.where(lane < q, roll(x, HALO - REACH - at_w), roll(x, 2 * q - HALO - at_e))
            dst[8 * t : 8 * t + 8, :] = out


def second_kernel(
    rows, half, cut, tail_cut, flags, s_a, s_b, r_a, r_b, corr, corr_s, gain, top, slope, mob, j0, j1,
    gain_s, top_s, slope_s, mob_s, j_s,
    end_own, end_send, d_a, d_b, g_a, g_b, corr_out,
    a0, a1, a_s, b0, b1, b_s, c0, c1, c_s, spread, folded, *work,
):
    lanes = a0.shape[1]
    q = lanes // 4
    h = flags[0]
    last = flags[1] == 1
    for ref in (a0, a1, a_s, b0, b1, b_s, c0, c1, c_s):
        clear_pads(ref, rows)
    folded[0:tail_cut, :] = s_a[cut:, :] + r_a[cut:, :]
    folded[tail_cut:, :] = s_b[rows - cut :, :] + r_b[rows - cut :, :]
    unfold(folded, spread, rows)

    def build(base, n):
        lane = lanes_of(n, lanes)
        here, padded = pl.ds(base, n), pl.ds(base + PAD, n)
        part, came, at = (s_a, r_a, base) if base < cut else (s_b, r_b, base - cut)
        s = part[pl.ds(at, n), :] + came[pl.ds(at, n), :]
        a0[padded, :] = s
        a1[padded, :] = gain[here, :] * s + corr[here, :]
        strip = spread[here, :]
        strip = jnp.where(inside(lane, (HALO, q)), roll(s, HALO), strip)
        strip = jnp.where(inside(lane, (q, 2 * q - HALO)), roll(s, 2 * q - HALO), strip)
        other = roll(gain_s[here, :] * strip + corr_s[here, :], 2 * q)
        a_s[padded, :] = jnp.where(lane < 2 * q, strip, other)

    over_chunks(rows, build)
    fine_steps(
        (
            ((a0, b0, c0, b0), top, slope, mob, j0),
            ((a1, b1, c1, b1), top, slope, mob, j1),
            ((a_s, b_s, c_s, b_s), top_s, slope_s, mob_s, j_s),
        ),
        rows,
        work,
    )

    def finish(base, n):
        lane = lanes_of(n, lanes)
        here = pl.ds(base, n)
        at = aligned(base + h * (rows - half))
        inner, padded = pl.ds(at, n), pl.ds(at + PAD, n)
        strip = b_s[padded, :]
        end0 = merge_edges(b0[padded, :], strip, 0, lane)
        end1 = merge_edges(b1[padded, :], strip, 1, lane)
        end_own[here, :] = jnp.where(h == 0, end0, end1) * 2.0
        end_send[here, :] = jnp.where(h == 0, end1, end0) * 2.0
        g = gain[inner, :]
        change = end0 - g * a0[padded, :]
        corr_out[here, :] = change * 2.0
        d_to, g_to, to = (d_a, g_a, base) if base < half // 2 else (d_b, g_b, base - half // 2)
        d_to[pl.ds(to, n), :] = jnp.where(last, end1, g * change + end1 - g * a1[padded, :]) * 2.0
        g_to[pl.ds(to, n), :] = g

    over_chunks(half, finish)


def stage_kernel(order, flags, g, d, came, out, passed):
    def body(base, n):
        here = pl.ds(base, n)
        gain = g[here, :]
        square = gain * gain
        fourth = square * square

        def weight(e):
            value = jnp.where(e % 2 == 1, square, 1.0) * jnp.where(e >= 2, fourth, 1.0)
            return jnp.where(e < 0, 0.0, value)

        mine, its = d[here, :], came[here, :]
        at = FLAGS + 3 * order
        out[here, :] = weight(flags[FLAGS - 1]) * mine + weight(flags[at]) * its
        passed[here, :] = weight(flags[at + 1]) * mine + weight(flags[at + 2]) * its

    over_chunks(d.shape[0], body)


def last_kernel(flags, s_a, s_b, r_a, r_b, g_a, g_b, corr, own, send):
    h = flags[0]
    tall = s_a.shape[0]
    for k, (s, r, g) in enumerate(((s_a, r_a, g_a), (s_b, r_b, g_b))):

        def body(base, n, k=k, s=s, r=r, g=g):
            here, there = pl.ds(base, n), pl.ds(base + k * tall, n)
            new0 = s[here, :] + r[here, :]
            new1 = g[here, :] * new0 + corr[there, :]
            own[there, :] = jnp.where(h == 0, new0, new1)
            send[there, :] = jnp.where(h == 0, new1, new0)

        over_chunks(tall, body)


def put_kernel(half, other, flags, piece, *rest):
    out, sem = rest[-2:]
    side = 1 - flags[0] if other else flags[0]
    copy = pltpu.make_async_copy(piece, out.at[pl.ds(aligned(side * half), half), :], sem)
    copy.start()
    copy.wait()


def put(half, flags, piece, into=None):
    anywhere = pl.BlockSpec(memory_space=pl.ANY)
    return pl.pallas_call(
        functools.partial(put_kernel, half, into is not None),
        out_shape=jax.ShapeDtypeStruct((2 * half, piece.shape[1]), jnp.float32),
        in_specs=[SMEM, VMEM] + ([anywhere] if into is not None else []),
        out_specs=anywhere,
        scratch_shapes=[pltpu.SemaphoreType.DMA],
        input_output_aliases={2: 0} if into is not None else {},
        compiler_params=PARAMS,
        cost_estimate=pl.CostEstimate(flops=0, bytes_accessed=piece.size * 8, transcendentals=0),
    )(flags, piece, *(() if into is None else (into,)))


def call(kernel, outs, scratch=(), smem=1, cost=None):
    def run(*operands):
        return pl.pallas_call(
            kernel,
            out_shape=[jax.ShapeDtypeStruct(shape, jnp.float32) for shape in outs],
            in_specs=[SMEM] * smem + [VMEM] * (len(operands) - smem),
            out_specs=[VMEM] * len(outs),
            scratch_shapes=[pltpu.VMEM(shape, jnp.float32) for shape in scratch],
            compiler_params=PARAMS,
            cost_estimate=cost,
        )(*operands)

    return run


def scan_plan(chips):
    levels = chips.bit_length() - 1
    every = range(chips)
    end = chips - 1
    own = [end if c == end else -1 for c in every]
    rising = []
    for b in range(levels):
        size = 1 << b
        into, keep, came = [], [], []
        for c in every:
            closes = (c >> (b + 1)) == (end >> (b + 1))
            if c & size:
                into.append(c % size)
                keep.append(0)
                came.append(-1 if closes else size)
            else:
                into.append(c if closes else -1)
                keep.append(-1 if closes else size)
                came.append(0)
        rising.append((b, into, keep, came))
    if levels != 2:
        return own, (rising, rising)

    def weight(to, at):
        return max(to - (at + 1) % chips, -1)

    both = []
    for one, two in ((1, 2), (2, 1)):
        first = [[weight(c, c ^ one) for c in every], [weight(c ^ two, c) for c in every]]
        first.append([weight(c ^ two, c ^ one) for c in every])
        both.append([(one.bit_length() - 1, *first), (two.bit_length() - 1,)])
    return own, tuple(both)


def power(square, exponents, chip):
    e = jnp.asarray(np.array(exponents, np.int32))[chip]
    value, factor = jnp.ones_like(square), square
    for k in range(max(max(exponents), 0).bit_length()):
        value = jnp.where((e >> k) & 1 == 1, value * factor, value)
        factor = factor * factor
    return jnp.where(e < 0, jnp.float32(0.0), value)


def exchange(value, bit, count):
    return lax.ppermute(value, "tm", [(i, i ^ (2 << bit)) for i in range(count)])


def scan(parts, gains, flags, chip, chips, count):
    own, orders = scan_plan(chips)
    if len(orders[0]) == 2:
        arrived = [exchange(d, order[0][0], count) for d, order in zip(parts, orders)]
        mid = [
            call(functools.partial(stage_kernel, p), (d.shape, d.shape))(flags, g, d, r)
            for p, (d, g, r) in enumerate(zip(parts, gains, arrived))
        ]
        came = [exchange(passed, order[1][0], count) for (_, passed), order in zip(mid, orders)]
        return [out for out, _ in mid], came
    squares = [g * g for g in gains]
    sums = [power(sq, own, chip) * d for sq, d in zip(squares, parts)]
    passed = list(parts)
    for stage in range(len(orders[0])):
        arrived = [exchange(d, order[stage][0], count) for d, order in zip(passed, orders)]
        for p, order in enumerate(orders):
            _, into, keep, came = order[stage]
            sums[p] = sums[p] + power(squares[p], into, chip) * arrived[p]
            passed[p] = power(squares[p], keep, chip) * passed[p] + power(squares[p], came, chip) * arrived[p]
    return sums, [jnp.zeros_like(x) for x in sums]


def local(initial_starts, source, region, base_reluctivity, saturation, mobility):
    potential, driver = initial_starts[0], source[0]
    radial, lanes = potential.shape
    count = lax.axis_size("tm")
    chips = count // 2
    spaces = lax.axis_size("space")
    slot = lax.axis_index("tm")
    chip = slot // 2
    half = radial // 2
    margin = -(-HALO // 8) * 8
    rows, start = half + margin, half - margin
    own, orders = scan_plan(chips)
    table = []
    for i in range(count):
        c = i // 2
        row = [i % 2, int(c == chips - 1), own[c]]
        for order in orders:
            row += [exponents[c] for exponents in order[0][1:]]
        table.append(row)
    flags = lax.dynamic_index_in_dim(jnp.asarray(np.array(table, np.int32)), slot, keepdims=False)
    tables = (base_reluctivity, saturation, mobility)
    partner = [(i, i ^ 1) for i in range(count)]
    slab, padded = (rows, lanes), (rows + 2 * PAD, lanes)
    cost = pl.CostEstimate(flops=240 * rows * lanes, bytes_accessed=40 * rows * lanes, transcendentals=0)

    there = (1 - slot % 2) * start
    send = jnp.concatenate(
        [lax.dynamic_slice(x, (there, 0), slab) for x in (potential, driver)], axis=0
    )
    got = lax.ppermute(send, "tm", partner)
    message = (rows // 2, lanes)
    a0, a1, j0, j1, to_west, to_east = call(
        functools.partial(pack_kernel, rows, start), (padded, padded, slab, slab, message, message), cost=cost
    )(flags, potential, driver, got, region)
    from_east = lax.ppermute(to_west, "space", [((i + 1) % spaces, i) for i in range(spaces)])
    from_west = lax.ppermute(to_east, "space", [(i, (i + 1) % spaces) for i in range(spaces)])
    f0, f1, top, slope, mob, gain, a_own, j_own, id_own = call(
        functools.partial(main_kernel, rows, start),
        (padded, padded) + (slab,) * 7, (padded,) * 12, smem=4, cost=cost,
    )(flags, *tables, region, a0, a1, j0, j1)

    tail = 8 * fold_tiles(rows)
    cut, tail_cut = rows // 2, 8 * (tail // 16)
    part_a, part_b = (cut + tail_cut, lanes), (rows - cut + tail - tail_cut, lanes)
    top_s, slope_s, mob_s, gain_s, j_s, corr, corr_s, d_a, d_b, g_a, g_b = call(
        functools.partial(strip_kernel, rows, cut, tail_cut),
        (slab,) * 7 + (part_a, part_b, part_a, part_b),
        (padded, padded, padded, slab, (tail, lanes)) + (padded,) * 4, smem=4, cost=cost,
    )(flags, *tables, from_west, from_east, a_own, j_own, id_own, a0, a1, f0, f1, gain)
    (s_a, s_b), (r_a, r_b) = scan((d_a, d_b), (g_a, g_b), flags, chip, chips, count)

    own_rows, quarter = (half, lanes), (half // 2, lanes)
    end_own, end_send, d_a, d_b, g_a, g_b, corr = call(
        functools.partial(second_kernel, rows, half, cut, tail_cut),
        (own_rows, own_rows, quarter, quarter, quarter, quarter, own_rows),
        (padded,) * 9 + (slab, (tail, lanes)) + (padded,) * 12, cost=cost,
    )(flags, s_a, s_b, r_a, r_b, corr, corr_s, gain, top, slope, mob, j0, j1, gain_s, top_s, slope_s, mob_s, j_s)
    end_got = lax.ppermute(end_send, "tm", partner)
    (s_a, s_b), (r_a, r_b) = scan((d_a, d_b), (g_a, g_b), flags, chip, chips, count)
    ends = put(half, flags, end_got, put(half, flags, end_own))
    new_own, new_send = call(last_kernel, (own_rows, own_rows))(flags, s_a, s_b, r_a, r_b, g_a, g_b, corr)
    new_got = lax.ppermute(new_send, "tm", partner)
    starts = put(half, flags, new_got, put(half, flags, new_own))
    return (starts[None], ends[None])


def solution(mesh):
    placed = (P("tm", None, "space"), P("tm", None, "space"), P(None, "space"), P(), P(), P())
    return jax.shard_map(
        local,
        mesh=mesh,
        in_specs=placed,
        out_specs=(P("tm", None, "space"), P("tm", None, "space")),
        check_vma=False,
    )
```

```python
import functools

import jax
import jax.numpy as jnp
import numpy as np
from jax import lax
from jax.experimental import pallas as pl
from jax.experimental.pallas import tpu as pltpu
from jax.sharding import PartitionSpec as P

STEPS = 3
ITERS = 2
HALO = 2 * STEPS * ITERS
J_HALO = HALO - 2
ID_HALO = HALO - 1
REACH = 2 * STEPS
PAD = 8
CHUNK = 96
FOLD = 8
VMEM = pl.BlockSpec(memory_space=pltpu.VMEM)
FLAGS = 3
SMEM = pl.BlockSpec(memory_space=pltpu.SMEM)
PARAMS = pltpu.CompilerParams(vmem_limit_bytes=14 * 1024 * 1024)


def lanes_of(rows, lanes):
    return lax.broadcasted_iota(jnp.int32, (rows, lanes), 1)


def roll(x, amount):
    amount = amount % x.shape[1]
    return pltpu.roll(x, amount, 1) if amount else x


def inside(lane, *spans):
    hit = None
    for low, high in spans:
        one = (lane >= low) & (lane < high)
        hit = one if hit is None else hit | one
    return hit


def pieces(rows):
    tiles = rows // 8
    count = -(-tiles // (CHUNK // 8))
    edges = [8 * (tiles * c // count) for c in range(count + 1)]
    return [(low, high - low) for low, high in zip(edges[:-1], edges[1:])]


def over_chunks(rows, body):
    for base, n in pieces(rows):
        body(base, n)


def aligned(at):
    return at if isinstance(at, int) else pl.multiple_of(at, 8)


def coefficients(region, nu_tab, sat_tab, mob_tab):
    base = jnp.zeros(region.shape, jnp.float32)
    satur, mobile = base, base
    for r in range(nu_tab.shape[0]):
        hit = region == r
        base = jnp.where(hit, nu_tab[r], base)
        satur = jnp.where(hit, sat_tab[r], satur)
        mobile = jnp.where(hit, mob_tab[r], mobile)
    gain = 1.0 / (1.0 + 12.0 * mobile * base)
    slope = base * satur
    return base + slope, slope, mobile * 0.5, gain


def fine_steps(units, rows, work, off=0):
    chunks = pieces(rows)
    for step in range(STEPS):
        moved = {}
        for turn in range(len(chunks) + 4):
            for u, (bufs, top, slope, mob, drive) in enumerate(units):
                old, new = bufs[step], bufs[step + 1]
                nu, east, flow, face = work[4 * u : 4 * u + 4]

                def place(c):
                    if not 0 <= c < len(chunks):
                        return None
                    base, n = chunks[c]
                    return pl.ds(base + PAD, n), pl.ds(base + PAD - 1, n), pl.ds(base + PAD + 1, n), pl.ds(aligned(off + base), n)

                c = turn - 3
                if spot := place(c):
                    at, above, _, _ = spot
                    nu0 = nu[at, :]
                    out = (nu0 + moved.pop((u, 3, c))) * east[at, :]
                    flow[at, :] = out
                    moved[u, 4, c] = roll(out, 1)
                    face[at, :] = (nu0 + nu[above, :]) * (old[at, :] - old[above, :])
                    if c == len(chunks) - 1:
                        end = PAD + rows
                        nu[end : end + 1, :] = nu[end - 1 : end, :]
                        at, above = pl.ds(end, 8), pl.ds(end - 1, 8)
                        face[at, :] = (nu[at, :] + nu[above, :]) * (old[at, :] - old[above, :])
                c = turn - 4
                if spot := place(c):
                    at, _, below, coef = spot
                    total = flow[at, :] - moved.pop((u, 4, c))
                    total = total + (face[below, :] - face[at, :])
                    new[at, :] = old[at, :] + mob[coef, :] * (total + drive[coef, :])
                c = turn - 2
                if spot := place(c):
                    at, above, below, coef = spot
                    dr = old[below, :] - old[above, :]
                    dt = east[at, :] + moved.pop((u, 2, c))
                    bottom = 1.0 + (dr * dr + dt * dt)
                    out = top[coef, :] - slope[coef, :] / bottom
                    nu[at, :] = out
                    if c == 0:
                        nu[PAD - 1 : PAD, :] = nu[PAD : PAD + 1, :]
                    moved[u, 3, c] = roll(out, -1)
                c = turn - 1
                if spot := place(c):
                    at = spot[0]
                    out = moved.pop((u, 1, c)) - old[at, :]
                    east[at, :] = out
                    moved[u, 2, c] = roll(out, 1)
                c = turn
                if spot := place(c):
                    moved[u, 1, c] = roll(old[spot[0], :], -1)


def clear_pads(ref, rows):
    ref[0:PAD, :] = jnp.zeros((PAD, ref.shape[1]), jnp.float32)
    ref[PAD + rows : rows + 2 * PAD, :] = jnp.zeros((PAD, ref.shape[1]), jnp.float32)


def pack_kernel(rows, start, flags, own_a, own_j, got, region, a0, a1, j0, j1, kind, to_west, to_east):
    lanes = a0.shape[1]
    q, both, tall = lanes // 4, HALO + J_HALO, rows // 2
    mine = flags[0] == 0
    first = flags[0] * start
    clear_pads(a0, rows)
    clear_pads(a1, rows)

    def body(low, n):
        lane = lanes_of(n, lanes)
        west = jnp.zeros((n, lanes), jnp.float32)
        east = west
        for k in range(2):
            base = low + k * tall
            src = pl.ds(aligned(first + base), n)
            a_own, j_own = own_a[src, :], own_j[src, :]
            a_got, j_got = got[pl.ds(base, n), :], got[pl.ds(base + rows, n), :]
            a_0, a_1 = jnp.where(mine, a_own, a_got) * 0.5, jnp.where(mine, a_got, a_own) * 0.5
            j_0, j_1 = jnp.where(mine, j_own, j_got), jnp.where(mine, j_got, j_own)
            a0[pl.ds(base + PAD, n), :] = a_0
            a1[pl.ds(base + PAD, n), :] = a_1
            j0[pl.ds(base, n), :] = j_0
            j1[pl.ds(base, n), :] = j_1
            ids = region[src, :].astype(jnp.float32)
            kind[pl.ds(base, n), :] = ids
            for s, (a, j) in enumerate(((a_0, j_0), (a_1, j_1))):
                at = (2 * s + 2) * q - HALO - k * both
                west = jnp.where(inside(lane, (at, at + HALO)), roll(a, at), west)
                at = at - J_HALO
                west = jnp.where(inside(lane, (at, at + J_HALO)), roll(j, at), west)
                at = 2 * s * q + k * both
                east = jnp.where(inside(lane, (at, at + HALO)), roll(a, at + HALO), east)
                at = at + HALO
                east = jnp.where(inside(lane, (at, at + J_HALO)), roll(j, at + J_HALO), east)
            at = 2 * q * (1 - k)
            west = jnp.where(inside(lane, (at, at + ID_HALO)), roll(ids, at), west)
            at = (3 - 2 * k) * q + HALO
            east = jnp.where(inside(lane, (at, at + ID_HALO)), roll(ids, at + ID_HALO), east)
        to_west[pl.ds(low, n), :] = west
        to_east[pl.ds(low, n), :] = east

    over_chunks(tall, body)


def own_part(s0, s1, lane):
    q = s0.shape[1] // 4
    out = jnp.zeros(s0.shape, jnp.float32)
    for s, x in enumerate((s0, s1)):
        w = 2 * s * q
        out = jnp.where(inside(lane, (w + HALO, w + q)), roll(x, w + HALO), out)
        out = jnp.where(inside(lane, (w + q, w + 2 * q - HALO)), roll(x, w + 2 * q - HALO), out)
    return out


def merge_edges(main, strip, s, lane):
    lanes = main.shape[1]
    q = lanes // 4
    w = 2 * s * q
    out = jnp.where(lane < REACH, roll(strip, -(w + HALO)), main)
    return jnp.where(lane >= lanes - REACH, roll(strip, -(w + 2 * q - HALO)), out)


def main_kernel(
    rows, flags, nu_tab, sat_tab, mob_tab, kind, a0, a1, j0, j1,
    f0, f1, top, slope, mob, gain, a_own, j_own, id_own, b0, c0, b1, c1, *work,
):
    for ref in (b0, c0, b1, c1):
        clear_pads(ref, rows)

    def body(base, n):
        lane = lanes_of(n, a0.shape[1])
        here, padded = pl.ds(base, n), pl.ds(base + PAD, n)
        top[here, :], slope[here, :], mob[here, :], gain[here, :] = coefficients(
            kind[here, :].astype(jnp.int32), nu_tab, sat_tab, mob_tab
        )
        a_own[here, :] = own_part(a0[padded, :], a1[padded, :], lane)
        j_own[here, :] = own_part(j0[here, :], j1[here, :], lane)
        id_own[here, :] = own_part(kind[here, :], kind[here, :], lane)

    over_chunks(rows, body)
    fine_steps((((a0, b0, c0, f0), top, slope, mob, j0), ((a1, b1, c1, f1), top, slope, mob, j1)), rows, work)


def strip_kernel(
    rows, span, flags, nu_tab, sat_tab, mob_tab, west, east, a_own, j_own, id_own,
    a0, a1, f0, f1, gain,
    top_s, slope_s, mob_s, gain_s, j_s, corr, corr_s, d_a, d_b, a_s, b_s, c_s, d_s, d_m, *work,
):
    lanes = a0.shape[1]
    q, both, tall = lanes // 4, HALO + J_HALO, rows // 2
    last = flags[1] == 1
    for ref in (a_s, b_s, c_s):
        clear_pads(ref, rows)

    def build(low, n):
        lane = lanes_of(n, lanes)
        heads = inside(lane, (0, HALO), (2 * q, 2 * q + HALO))
        tails = inside(lane, (2 * q - HALO, 2 * q), (4 * q - HALO, 4 * q))
        w, e = west[pl.ds(low, n), :], east[pl.ds(low, n), :]
        w_ids = roll(w, 1 - (3 * q + HALO)), roll(w, 1 - (q + HALO))
        e_ids = roll(e, -HALO), roll(e, 2 * q - HALO)
        for k in range(2):
            base = low + k * tall
            here, padded = pl.ds(base, n), pl.ds(base + PAD, n)

            def halo(from_west, from_east, rest):
                return jnp.where(heads, from_west, jnp.where(tails, from_east, rest))

            a_s[padded, :] = halo(roll(w, -both) if k else w, roll(e, both) if k else e, a_own[here, :])
            j_s[here, :] = halo(
                roll(w, -J_HALO - k * both), roll(e, J_HALO + k * both), j_own[here, :]
            )
            lower = lane < 2 * q
            ids = halo(
                jnp.where(lower, w_ids[k], w_ids[1 - k]), jnp.where(lower, e_ids[k], e_ids[1 - k]), id_own[here, :]
            )
            top_s[here, :], slope_s[here, :], mob_s[here, :], gain_s[here, :] = coefficients(
                ids.astype(jnp.int32), nu_tab, sat_tab, mob_tab
            )

    over_chunks(tall, build)
    fine_steps((((a_s, b_s, c_s, b_s), top_s, slope_s, mob_s, j_s),), rows, work)

    def finish(base, n):
        lane = lanes_of(n, lanes)
        here, padded = pl.ds(base, n), pl.ds(base + PAD, n)
        strip = b_s[padded, :]
        g_s = gain_s[here, :]
        c = strip - g_s * a_s[padded, :]
        corr_s[here, :] = c
        d_s[here, :] = roll(jnp.where(last, strip, c), 2 * q) + jnp.where(last, 0.0, g_s * c)
        g = gain[here, :]
        end0 = merge_edges(f0[padded, :], strip, 0, lane)
        end1 = merge_edges(f1[padded, :], strip, 1, lane)
        change = end0 - g * a0[padded, :]
        corr[here, :] = change
        d_m[here, :] = jnp.where(last, end1, g * change + end1 - g * a1[padded, :])

    over_chunks(rows, finish)
    for p, out in enumerate((d_a, d_b)):
        off = part_start(flags, p, rows)
        out[0:span, :] = d_m[pl.ds(off, span), :]
        fold(d_s, off, out, span, span)


def part_start(flags, p, rows):
    half = rows - 2 * PAD
    return aligned(PAD * flags[0] + p * (half // 2 - PAD))


def fold_kernel(rows, span, flags, gain_s, g_a, g_b):
    for p, out in enumerate((g_a, g_b)):
        fold(gain_s, part_start(flags, p, rows), out, span, 0)


def fold_tiles(rows):
    return -(-(rows // 8) // FOLD)


def fold(src, off, dst, rows, to):
    lanes = src.shape[1]
    q, width = lanes // 4, lanes // FOLD
    lane = lanes_of(8, lanes)
    tiles = fold_tiles(rows)
    for r in range(tiles):
        out = jnp.zeros((8, lanes), jnp.float32)
        for k in range(FOLD):
            t = k * tiles + r
            if 8 * t >= rows:
                continue
            x = src[pl.ds(aligned(off + 8 * t), 8), :]
            at_w, at_e = width * k, width * k + width // 2
            out = jnp.where(inside(lane, (at_w, at_w + REACH)), roll(x, at_w - (HALO - REACH)), out)
            out = jnp.where(inside(lane, (at_e, at_e + REACH)), roll(x, at_e - (2 * q - HALO)), out)
        dst[to + 8 * r : to + 8 * r + 8, :] = out


def unfold(src, dst, rows):
    lanes = src.shape[1]
    q, width = lanes // 4, lanes // FOLD
    lane = lanes_of(8, lanes)
    tiles = fold_tiles(rows)
    for r in range(tiles):
        x = src[8 * r : 8 * r + 8, :]
        for k in range(FOLD):
            t = k * tiles + r
            if 8 * t >= rows:
                continue
            at_w, at_e = width * k, width * k + width // 2
            out = jnp.where(lane < q, roll(x, HALO - REACH - at_w), roll(x, 2 * q - HALO - at_e))
            dst[8 * t : 8 * t + 8, :] = out


def second_kernel(
    rows, span, p, flags, sums, came, corr, corr_s, gain, top, slope, mob, j0, j1,
    gain_s, top_s, slope_s, mob_s, j_s,
    end_own, end_send, d_out, corr_out, a0, a1, a_s, b0, b1, b_s, c0, c1, c_s, spread, folded, *work,
):
    lanes = a0.shape[1]
    q = lanes // 4
    h = flags[0]
    last = flags[1] == 1
    off = part_start(flags, p, rows)
    for ref in (a0, a1, a_s, b0, b1, b_s, c0, c1, c_s):
        clear_pads(ref, span)
    folded[...] = sums[span:, :] + came[span:, :]
    unfold(folded, spread, span)

    def build(base, n):
        lane = lanes_of(n, lanes)
        here, padded, slab = pl.ds(base, n), pl.ds(base + PAD, n), pl.ds(aligned(off + base), n)
        s = sums[here, :] + came[here, :]
        a0[padded, :] = s
        a1[padded, :] = gain[slab, :] * s + corr[slab, :]
        strip = spread[here, :]
        strip = jnp.where(inside(lane, (HALO, q)), roll(s, HALO), strip)
        strip = jnp.where(inside(lane, (q, 2 * q - HALO)), roll(s, 2 * q - HALO), strip)
        other = roll(gain_s[slab, :] * strip + corr_s[slab, :], 2 * q)
        a_s[padded, :] = jnp.where(lane < 2 * q, strip, other)

    over_chunks(span, build)
    fine_steps(
        (
            ((a0, b0, c0, b0), top, slope, mob, j0),
            ((a1, b1, c1, b1), top, slope, mob, j1),
            ((a_s, b_s, c_s, b_s), top_s, slope_s, mob_s, j_s),
        ),
        span,
        work,
        off,
    )

    def finish(base, n):
        lane = lanes_of(n, lanes)
        here = pl.ds(base, n)
        at = PAD * (h + p) + base
        padded, slab = pl.ds(aligned(at + PAD), n), pl.ds(aligned(off + at), n)
        strip = b_s[padded, :]
        end0 = merge_edges(b0[padded, :], strip, 0, lane)
        end1 = merge_edges(b1[padded, :], strip, 1, lane)
        end_own[here, :] = jnp.where(h == 0, end0, end1) * 2.0
        end_send[here, :] = jnp.where(h == 0, end1, end0) * 2.0
        g = gain[slab, :]
        change = end0 - g * a0[padded, :]
        corr_out[here, :] = change * 2.0
        d_out[here, :] = jnp.where(last, end1, g * change + end1 - g * a1[padded, :]) * 2.0

    over_chunks(span - 2 * PAD, finish)


def own_start(flags, p, rows):
    return aligned(part_start(flags, p, rows) + PAD * (flags[0] + p))


def stage_kernel(rows, p, flags, gain, d, came, *rest):
    out, passed = rest[-2:]
    tail = rest[0].shape[0] if len(rest) == 3 else 0
    body_rows = d.shape[0] - tail
    off = part_start(flags, p, rows) if tail else own_start(flags, p, rows)

    def weight(e, square, fourth):
        value = jnp.where(e % 2 == 1, square, 1.0) * jnp.where(e >= 2, fourth, 1.0)
        return jnp.where(e < 0, 0.0, value)

    def one(here, g):
        square = g * g
        fourth = square * square
        mine, its = d[here, :], came[here, :]
        at = FLAGS + 3 * p
        out[here, :] = weight(flags[FLAGS - 1], square, fourth) * mine + weight(flags[at], square, fourth) * its
        passed[here, :] = weight(flags[at + 1], square, fourth) * mine + weight(flags[at + 2], square, fourth) * its

    over_chunks(body_rows, lambda base, n: one(pl.ds(base, n), gain[pl.ds(aligned(off + base), n), :]))
    if tail:
        one(pl.ds(body_rows, tail), rest[0][...])


def last_kernel(rows, p, flags, sums, came, gain, corr, own, send):
    h = flags[0]
    off = own_start(flags, p, rows)

    def body(base, n):
        here = pl.ds(base, n)
        new0 = sums[here, :] + came[here, :]
        new1 = gain[pl.ds(aligned(off + base), n), :] * new0 + corr[here, :]
        own[here, :] = jnp.where(h == 0, new0, new1)
        send[here, :] = jnp.where(h == 0, new1, new0)

    over_chunks(sums.shape[0], body)


def put_kernel(half, places, flags, *refs):
    out, sems = refs[-2:]
    copies = []
    for i, (other, p) in enumerate(places):
        side = 1 - flags[0] if other else flags[0]
        to = out.at[pl.ds(aligned(side * half + p * (half // 2)), half // 2), :]
        copies.append(pltpu.make_async_copy(refs[i], to, sems.at[i]))
        copies[-1].start()
    for copy in copies:
        copy.wait()


def put(half, places, flags, parts, into=None):
    anywhere = pl.BlockSpec(memory_space=pl.ANY)
    count = len(parts)
    return pl.pallas_call(
        functools.partial(put_kernel, half, places),
        out_shape=jax.ShapeDtypeStruct((2 * half, parts[0].shape[1]), jnp.float32),
        in_specs=[SMEM] + [VMEM] * count + ([anywhere] if into is not None else []),
        out_specs=anywhere,
        scratch_shapes=[pltpu.SemaphoreType.DMA((count,))],
        input_output_aliases={count + 1: 0} if into is not None else {},
        compiler_params=PARAMS,
        cost_estimate=pl.CostEstimate(flops=0, bytes_accessed=count * parts[0].size * 8, transcendentals=0),
    )(flags, *parts, *(() if into is None else (into,)))


def call(kernel, outs, scratch=(), smem=1, cost=None):
    def run(*operands):
        return pl.pallas_call(
            kernel,
            out_shape=[jax.ShapeDtypeStruct(shape, jnp.float32) for shape in outs],
            in_specs=[SMEM] * smem + [VMEM] * (len(operands) - smem),
            out_specs=[VMEM] * len(outs),
            scratch_shapes=[pltpu.VMEM(shape, jnp.float32) for shape in scratch],
            compiler_params=PARAMS,
            cost_estimate=cost,
        )(*operands)

    return run


def scan_plan(chips):
    levels = chips.bit_length() - 1
    every = range(chips)
    end = chips - 1
    own = [end if c == end else -1 for c in every]
    rising = []
    for b in range(levels):
        size = 1 << b
        into, keep, came = [], [], []
        for c in every:
            closes = (c >> (b + 1)) == (end >> (b + 1))
            if c & size:
                into.append(c % size)
                keep.append(0)
                came.append(-1 if closes else size)
            else:
                into.append(c if closes else -1)
                keep.append(-1 if closes else size)
                came.append(0)
        rising.append((b, into, keep, came))
    if levels != 2:
        return own, (rising, rising)

    def weight(to, at):
        return max(to - (at + 1) % chips, -1)

    both = []
    for one, two in ((1, 2), (2, 1)):
        first = [[weight(c, c ^ one) for c in every], [weight(c ^ two, c) for c in every]]
        first.append([weight(c ^ two, c ^ one) for c in every])
        both.append([(one.bit_length() - 1, *first), (two.bit_length() - 1,)])
    return own, tuple(both)


def power(square, exponents, chip):
    e = jnp.asarray(np.array(exponents, np.int32))[chip]
    value, factor = jnp.ones_like(square), square
    for k in range(max(max(exponents), 0).bit_length()):
        value = jnp.where((e >> k) & 1 == 1, value * factor, value)
        factor = factor * factor
    return jnp.where(e < 0, jnp.float32(0.0), value)


def exchange(value, bit, count):
    return lax.ppermute(value, "tm", [(i, i ^ (2 << bit)) for i in range(count)])


def scan(parts, gain, folds, rows, flags, chip, chips, count):
    own, orders = scan_plan(chips)
    if len(orders[0]) == 2:
        arrived = [exchange(d, order[0][0], count) for d, order in zip(parts, orders)]
        mid = [
            call(functools.partial(stage_kernel, rows, p), (d.shape, d.shape))(flags, gain, d, r, *fold)
            for p, (d, r, fold) in enumerate(zip(parts, arrived, folds))
        ]
        came = [exchange(passed, order[1][0], count) for (_, passed), order in zip(mid, orders)]
        return [out for out, _ in mid], came
    squares = []
    for p, (d, fold) in enumerate(zip(parts, folds)):
        plain = d.shape[0] - sum(f.shape[0] for f in fold)
        off = PAD * flags[0] + p * ((rows - 2 * PAD) // 2 - PAD)
        if not fold:
            off = off + PAD * (flags[0] + p)
        g = jnp.concatenate([lax.dynamic_slice(gain, (off, 0), (plain, d.shape[1])), *fold], axis=0)
        squares.append(g * g)
    sums = [power(sq, own, chip) * d for sq, d in zip(squares, parts)]
    passed = list(parts)
    for stage in range(len(orders[0])):
        arrived = [exchange(d, order[stage][0], count) for d, order in zip(passed, orders)]
        for p, order in enumerate(orders):
            _, into, keep, came = order[stage]
            sums[p] = sums[p] + power(squares[p], into, chip) * arrived[p]
            passed[p] = power(squares[p], keep, chip) * passed[p] + power(squares[p], came, chip) * arrived[p]
    return sums, [jnp.zeros_like(x) for x in sums]


def local(initial_starts, source, region, base_reluctivity, saturation, mobility):
    potential, driver = initial_starts[0], source[0]
    radial, lanes = potential.shape
    count = lax.axis_size("tm")
    chips = count // 2
    spaces = lax.axis_size("space")
    slot = lax.axis_index("tm")
    chip = slot // 2
    half = radial // 2
    margin = -(-HALO // 8) * 8
    rows, start = half + margin, half - margin
    own, orders = scan_plan(chips)
    table = []
    for i in range(count):
        c = i // 2
        row = [i % 2, int(c == chips - 1), own[c]]
        for order in orders:
            row += [exponents[c] for exponents in order[0][1:]]
        table.append(row)
    flags = lax.dynamic_index_in_dim(jnp.asarray(np.array(table, np.int32)), slot, keepdims=False)
    tables = (base_reluctivity, saturation, mobility)
    partner = [(i, i ^ 1) for i in range(count)]
    slab, padded = (rows, lanes), (rows + 2 * PAD, lanes)
    cost = pl.CostEstimate(flops=240 * rows * lanes, bytes_accessed=40 * rows * lanes, transcendentals=0)

    there = (1 - slot % 2) * start
    send = jnp.concatenate(
        [lax.dynamic_slice(x, (there, 0), slab) for x in (potential, driver)], axis=0
    )
    got = lax.ppermute(send, "tm", partner)
    message = (rows // 2, lanes)
    a0, a1, j0, j1, kind, to_west, to_east = call(
        functools.partial(pack_kernel, rows, start), (padded, padded, slab, slab, slab, message, message), cost=cost
    )(flags, potential, driver, got, region)
    from_east = lax.ppermute(to_west, "space", [((i + 1) % spaces, i) for i in range(spaces)])
    from_west = lax.ppermute(to_east, "space", [(i, (i + 1) % spaces) for i in range(spaces)])
    f0, f1, top, slope, mob, gain, a_own, j_own, id_own = call(
        functools.partial(main_kernel, rows), (padded, padded) + (slab,) * 7, (padded,) * 12, smem=4, cost=cost
    )(flags, *tables, kind, a0, a1, j0, j1)

    span = half // 2 + 2 * PAD
    tail = 8 * fold_tiles(span)
    part = (span + tail, lanes)
    top_s, slope_s, mob_s, gain_s, j_s, corr, corr_s, *sums = call(
        functools.partial(strip_kernel, rows, span),
        (slab,) * 7 + (part, part), (padded, padded, padded, slab, slab) + (padded,) * 4, smem=4, cost=cost,
    )(flags, *tables, from_west, from_east, a_own, j_own, id_own, a0, a1, f0, f1, gain)
    folds = call(functools.partial(fold_kernel, rows, span), ((tail, lanes),) * 2)(flags, gain_s)
    sums, came = scan(sums, gain, [(f,) for f in folds], rows, flags, chip, chips, count)

    quarter, room = (half // 2, lanes), (span + 2 * PAD, lanes)
    ends, starts, sums_2, corrs = [], [], [], []
    for p in range(2):
        end_own, end_send, d, change = call(
            functools.partial(second_kernel, rows, span, p),
            (quarter,) * 4, (room,) * 9 + ((span, lanes), (tail, lanes)) + (room,) * 12, cost=cost,
        )(flags, sums[p], came[p], corr, corr_s, gain, top, slope, mob, j0, j1, gain_s, top_s, slope_s, mob_s, j_s)
        ends += [end_own, lax.ppermute(end_send, "tm", partner)]
        sums_2.append(d)
        corrs.append(change)
    places = ((0, 0), (1, 0), (0, 1), (1, 1))
    sums, came = scan(sums_2, gain, [(), ()], rows, flags, chip, chips, count)
    ends = put(half, places, flags, ends)
    for p in range(2):
        if p == 1:
            flags, ends = lax.optimization_barrier((flags, ends))
        new_own, new_send = call(functools.partial(last_kernel, rows, p), (quarter, quarter))(
            flags, sums[p], came[p], gain, corrs[p]
        )
        starts += [new_own, lax.ppermute(new_send, "tm", partner)]
    starts = put(half, places[3:], flags, starts[3:], put(half, places[:3], flags, starts[:3]))
    return (starts[None], ends[None])


def solution(mesh):
    placed = (P("tm", None, "space"), P("tm", None, "space"), P(None, "space"), P(), P(), P())
    return jax.shard_map(
        local,
        mesh=mesh,
        in_specs=placed,
        out_specs=(P("tm", None, "space"), P("tm", None, "space")),
        check_vma=False,
    )
```

```python
import functools

import jax
import jax.numpy as jnp
import numpy as np
from jax import lax
from jax.experimental import pallas as pl
from jax.experimental.pallas import tpu as pltpu
from jax.sharding import PartitionSpec as P

STEPS = 3
ITERS = 2
HALO = 2 * STEPS * ITERS
J_HALO = HALO - 2
ID_HALO = HALO - 1
REACH = 2 * STEPS
PAD = 8
CHUNK = 96
FOLD = 8
VMEM = pl.BlockSpec(memory_space=pltpu.VMEM)
PARAMS = pltpu.CompilerParams(vmem_limit_bytes=14 * 1024 * 1024)


def place(chips):
    slot = lax.axis_index("tm")
    chip = slot // 2
    return slot % 2, chip, chip == chips - 1


def lanes_of(rows, lanes):
    return lax.broadcasted_iota(jnp.int32, (rows, lanes), 1)


def roll(x, amount):
    amount = amount % x.shape[1]
    return pltpu.roll(x, amount, 1) if amount else x


def inside(lane, *spans):
    hit = None
    for low, high in spans:
        one = (lane >= low) & (lane < high)
        hit = one if hit is None else hit | one
    return hit


def pieces(rows):
    tiles = rows // 8
    count = -(-tiles // (CHUNK // 8))
    edges = [8 * (tiles * c // count) for c in range(count + 1)]
    return [(low, high - low) for low, high in zip(edges[:-1], edges[1:])]


def over_chunks(rows, body):
    for base, n in pieces(rows):
        body(base, n)


def aligned(at):
    return at if isinstance(at, int) else pl.multiple_of(at, 8)


def coefficients(kind, table):
    regions = table.shape[0] // 3
    base, satur, mobile = (table[t * regions : t * regions + 1, :] for t in range(3))
    base, satur, mobile = (jnp.broadcast_to(x, kind.shape) for x in (base, satur, mobile))
    for r in range(1, regions):
        hit = kind == r
        base = jnp.where(hit, table[r : r + 1, :], base)
        satur = jnp.where(hit, table[regions + r : regions + r + 1, :], satur)
        mobile = jnp.where(hit, table[2 * regions + r : 2 * regions + r + 1, :], mobile)
    gain = 1.0 / (1.0 + 12.0 * mobile * base)
    slope = base * satur
    return base + slope, slope, mobile * 0.5, gain


def fine_steps(units, rows, work):
    chunks = pieces(rows)
    for step in range(STEPS):
        moved = {}
        for turn in range(len(chunks) + 4):
            for u, (bufs, top, slope, mob, drive, *skip) in enumerate(units):
                off = skip[0] if skip else 0
                old, new = bufs[step], bufs[step + 1]
                nu, east, flow, face = work[4 * u : 4 * u + 4]

                def rows_of(c, off=off):
                    if not 0 <= c < len(chunks):
                        return None
                    base, n = chunks[c]
                    return pl.ds(base + PAD, n), pl.ds(base + PAD - 1, n), pl.ds(base + PAD + 1, n), pl.ds(aligned(off + base), n)

                c = turn - 3
                if spot := rows_of(c):
                    at, above, _, _ = spot
                    nu0 = nu[at, :]
                    out = (nu0 + moved.pop((u, 3, c))) * east[at, :]
                    flow[at, :] = out
                    moved[u, 4, c] = roll(out, 1)
                    face[at, :] = (nu0 + nu[above, :]) * (old[at, :] - old[above, :])
                    if c == len(chunks) - 1:
                        end = PAD + rows
                        nu[end : end + 1, :] = nu[end - 1 : end, :]
                        at, above = pl.ds(end, 8), pl.ds(end - 1, 8)
                        face[at, :] = (nu[at, :] + nu[above, :]) * (old[at, :] - old[above, :])
                c = turn - 4
                if spot := rows_of(c):
                    at, _, below, coef = spot
                    total = flow[at, :] - moved.pop((u, 4, c))
                    total = total + (face[below, :] - face[at, :])
                    new[at, :] = old[at, :] + mob[coef, :] * (total + drive[coef, :])
                c = turn - 2
                if spot := rows_of(c):
                    at, above, below, coef = spot
                    dr = old[below, :] - old[above, :]
                    dt = east[at, :] + moved.pop((u, 2, c))
                    bottom = 1.0 + (dr * dr + dt * dt)
                    out = top[coef, :] - slope[coef, :] / bottom
                    nu[at, :] = out
                    if c == 0:
                        nu[PAD - 1 : PAD, :] = nu[PAD : PAD + 1, :]
                    moved[u, 3, c] = roll(out, -1)
                c = turn - 1
                if spot := rows_of(c):
                    at = spot[0]
                    out = moved.pop((u, 1, c)) - old[at, :]
                    east[at, :] = out
                    moved[u, 2, c] = roll(out, 1)
                c = turn
                if spot := rows_of(c):
                    moved[u, 1, c] = roll(old[spot[0], :], -1)


def clear_pads(ref, rows):
    ref[0:PAD, :] = jnp.zeros((PAD, ref.shape[1]), jnp.float32)
    ref[PAD + rows : rows + 2 * PAD, :] = jnp.zeros((PAD, ref.shape[1]), jnp.float32)


def pack_kernel(rows, start, chips, own_a, own_j, got, region, a0, a1, j0, j1, kind, to_west, to_east):
    lanes = a0.shape[1]
    q, both = lanes // 4, HALO + J_HALO
    h, _, _ = place(chips)
    mine = h == 0
    first = h * start
    clear_pads(a0, rows)
    clear_pads(a1, rows)

    def gather(base, n):
        src = pl.ds(aligned(first + base), n)
        a_own, j_own = own_a[src, :] * 0.5, own_j[src, :]
        a_got, j_got = got[pl.ds(base, n), :] * 0.5, got[pl.ds(base + rows, n), :]
        here, padded = pl.ds(base, n), pl.ds(base + PAD, n)
        a0[padded, :], a1[padded, :] = jnp.where(mine, a_own, a_got), jnp.where(mine, a_got, a_own)
        j0[here, :], j1[here, :] = jnp.where(mine, j_own, j_got), jnp.where(mine, j_got, j_own)
        kind[here, :] = region[src, :].astype(jnp.float32)

    over_chunks(rows, gather)

    def body(low, n):
        lane = lanes_of(n, lanes)
        west = jnp.zeros((n, lanes), jnp.float32)
        east = west
        for k in range(2):
            base = part_start(h, k, rows) + low
            here, padded = pl.ds(aligned(base), n), pl.ds(aligned(base + PAD), n)
            ids = kind[here, :]
            for s, (a, j) in enumerate(((a0[padded, :], j0[here, :]), (a1[padded, :], j1[here, :]))):
                at = (2 * s + 2) * q - HALO - k * both
                west = jnp.where(inside(lane, (at, at + HALO)), roll(a, at), west)
                at = at - J_HALO
                west = jnp.where(inside(lane, (at, at + J_HALO)), roll(j, at), west)
                at = 2 * s * q + k * both
                east = jnp.where(inside(lane, (at, at + HALO)), roll(a, at + HALO), east)
                at = at + HALO
                east = jnp.where(inside(lane, (at, at + J_HALO)), roll(j, at + J_HALO), east)
            at = 2 * q * (1 - k)
            west = jnp.where(inside(lane, (at, at + ID_HALO)), roll(ids, at), west)
            at = (3 - 2 * k) * q + HALO
            east = jnp.where(inside(lane, (at, at + ID_HALO)), roll(ids, at + ID_HALO), east)
        to_west[pl.ds(low, n), :] = west
        to_east[pl.ds(low, n), :] = east

    over_chunks(to_west.shape[0], body)


def own_part(s0, s1, lane):
    q = s0.shape[1] // 4
    out = jnp.zeros(s0.shape, jnp.float32)
    for s, x in enumerate((s0, s1)):
        w = 2 * s * q
        out = jnp.where(inside(lane, (w + HALO, w + q)), roll(x, w + HALO), out)
        out = jnp.where(inside(lane, (w + q, w + 2 * q - HALO)), roll(x, w + 2 * q - HALO), out)
    return out


def merge_edges(main, strip, s, lane):
    lanes = main.shape[1]
    q = lanes // 4
    w = 2 * s * q
    out = jnp.where(lane < REACH, roll(strip, -(w + HALO)), main)
    return jnp.where(lane >= lanes - REACH, roll(strip, -(w + 2 * q - HALO)), out)


def main_kernel(
    rows, table, kind, a0, a1, j0, j1,
    f0, f1, top, slope, mob, gain, a_own, j_own, id_own, b0, c0, b1, c1, *work,
):
    for ref in (b0, c0, b1, c1):
        clear_pads(ref, rows)

    def body(base, n):
        lane = lanes_of(n, a0.shape[1])
        here, padded = pl.ds(base, n), pl.ds(base + PAD, n)
        top[here, :], slope[here, :], mob[here, :], gain[here, :] = coefficients(kind[here, :], table)
        a_own[here, :] = own_part(a0[padded, :], a1[padded, :], lane)
        j_own[here, :] = own_part(j0[here, :], j1[here, :], lane)
        id_own[here, :] = own_part(kind[here, :], kind[here, :], lane)

    over_chunks(rows, body)
    fine_steps((((a0, b0, c0, f0), top, slope, mob, j0), ((a1, b1, c1, f1), top, slope, mob, j1)), rows, work)


def strip_kernel(
    rows, span, p, chips, table, west, east, a_own, j_own, id_own, a0, a1, f0, f1, gain,
    d_out, corr, corr_s, top_s, slope_s, mob_s, gain_s, j_s, a_s, b_s, c_s, d_s, *work,
):
    lanes = a0.shape[1]
    q, both = lanes // 4, HALO + J_HALO
    h, _, last = place(chips)
    off = part_start(h, p, rows)
    for ref in (a_s, b_s, c_s):
        clear_pads(ref, span)

    def build(base, n):
        lane = lanes_of(n, lanes)
        heads = inside(lane, (0, HALO), (2 * q, 2 * q + HALO))
        tails = inside(lane, (2 * q - HALO, 2 * q), (4 * q - HALO, 4 * q))
        here, padded, slab = pl.ds(base, n), pl.ds(base + PAD, n), pl.ds(aligned(off + base), n)
        w, e = west[here, :], east[here, :]
        w_ids = roll(w, 1 - (3 * q + HALO)), roll(w, 1 - (q + HALO))
        e_ids = roll(e, -HALO), roll(e, 2 * q - HALO)

        def halo(from_west, from_east, rest):
            return jnp.where(heads, from_west, jnp.where(tails, from_east, rest))

        a_s[padded, :] = halo(roll(w, -p * both), roll(e, p * both), a_own[slab, :])
        j_s[here, :] = halo(roll(w, -J_HALO - p * both), roll(e, J_HALO + p * both), j_own[slab, :])
        lower = lane < 2 * q
        kind = halo(
            jnp.where(lower, w_ids[p], w_ids[1 - p]), jnp.where(lower, e_ids[p], e_ids[1 - p]), id_own[slab, :]
        )
        top_s[here, :], slope_s[here, :], mob_s[here, :], gain_s[here, :] = coefficients(kind, table)

    over_chunks(span, build)
    fine_steps((((a_s, b_s, c_s, b_s), top_s, slope_s, mob_s, j_s),), span, work)

    def finish(base, n):
        lane = lanes_of(n, lanes)
        here, padded = pl.ds(base, n), pl.ds(base + PAD, n)
        slab, deep = pl.ds(aligned(off + base), n), pl.ds(aligned(off + base + PAD), n)
        strip = b_s[padded, :]
        g_s = gain_s[here, :]
        c = strip - g_s * a_s[padded, :]
        corr_s[here, :] = c
        d_s[here, :] = roll(jnp.where(last, strip, c), 2 * q) + jnp.where(last, 0.0, g_s * c)
        g = gain[slab, :]
        end0 = merge_edges(f0[deep, :], strip, 0, lane)
        end1 = merge_edges(f1[deep, :], strip, 1, lane)
        change = end0 - g * a0[deep, :]
        corr[here, :] = change
        d_out[here, :] = jnp.where(last, end1, g * change + end1 - g * a1[deep, :])

    over_chunks(span, finish)
    fold(d_s, d_out, span, span)


def part_start(h, p, rows):
    return aligned(PAD * h + p * ((rows - 2 * PAD) // 2 - PAD))


def fold_kernel(span, gain_s, out):
    fold(gain_s, out, span, 0)


def fold_tiles(rows):
    return -(-(rows // 8) // FOLD)


def fold(src, dst, rows, to):
    lanes = src.shape[1]
    q, width = lanes // 4, lanes // FOLD
    lane = lanes_of(8, lanes)
    tiles = fold_tiles(rows)
    for r in range(tiles):
        out = jnp.zeros((8, lanes), jnp.float32)
        for k in range(FOLD):
            t = k * tiles + r
            if 8 * t >= rows:
                continue
            x = src[8 * t : 8 * t + 8, :]
            at_w, at_e = width * k, width * k + width // 2
            out = jnp.where(inside(lane, (at_w, at_w + REACH)), roll(x, at_w - (HALO - REACH)), out)
            out = jnp.where(inside(lane, (at_e, at_e + REACH)), roll(x, at_e - (2 * q - HALO)), out)
        dst[to + 8 * r : to + 8 * r + 8, :] = out


def unfold(src, dst, rows):
    lanes = src.shape[1]
    q, width = lanes // 4, lanes // FOLD
    lane = lanes_of(8, lanes)
    tiles = fold_tiles(rows)
    for r in range(tiles):
        x = src[8 * r : 8 * r + 8, :]
        for k in range(FOLD):
            t = k * tiles + r
            if 8 * t >= rows:
                continue
            at_w, at_e = width * k, width * k + width // 2
            out = jnp.where(lane < q, roll(x, HALO - REACH - at_w), roll(x, 2 * q - HALO - at_e))
            dst[8 * t : 8 * t + 8, :] = out


def second_kernel(
    rows, span, p, chips, sums, came, corr, corr_s, gain, top, slope, mob, j0, j1,
    gain_s, top_s, slope_s, mob_s, j_s,
    end_own, end_send, d_out, corr_out, a0, a1, a_s, b0, b1, b_s, c0, c1, c_s, spread, folded, *work,
):
    lanes = a0.shape[1]
    q = lanes // 4
    h, _, last = place(chips)
    off = part_start(h, p, rows)
    for ref in (a0, a1, a_s, b0, b1, b_s, c0, c1, c_s):
        clear_pads(ref, span)
    folded[...] = sums[span:, :] + came[span:, :]
    unfold(folded, spread, span)

    def build(base, n):
        lane = lanes_of(n, lanes)
        here, padded, slab = pl.ds(base, n), pl.ds(base + PAD, n), pl.ds(aligned(off + base), n)
        s = sums[here, :] + came[here, :]
        a0[padded, :] = s
        a1[padded, :] = gain[slab, :] * s + corr[here, :]
        strip = spread[here, :]
        strip = jnp.where(inside(lane, (HALO, q)), roll(s, HALO), strip)
        strip = jnp.where(inside(lane, (q, 2 * q - HALO)), roll(s, 2 * q - HALO), strip)
        other = roll(gain_s[here, :] * strip + corr_s[here, :], 2 * q)
        a_s[padded, :] = jnp.where(lane < 2 * q, strip, other)

    over_chunks(span, build)
    fine_steps(
        (
            ((a0, b0, c0, b0), top, slope, mob, j0, off),
            ((a1, b1, c1, b1), top, slope, mob, j1, off),
            ((a_s, b_s, c_s, b_s), top_s, slope_s, mob_s, j_s, 0),
        ),
        span,
        work,
    )

    def finish(base, n):
        lane = lanes_of(n, lanes)
        here = pl.ds(base, n)
        at = PAD * (h + p) + base
        padded, slab = pl.ds(aligned(at + PAD), n), pl.ds(aligned(off + at), n)
        strip = b_s[padded, :]
        end0 = merge_edges(b0[padded, :], strip, 0, lane)
        end1 = merge_edges(b1[padded, :], strip, 1, lane)
        end_own[here, :] = jnp.where(h == 0, end0, end1) * 2.0
        end_send[here, :] = jnp.where(h == 0, end1, end0) * 2.0
        g = gain[slab, :]
        change = end0 - g * a0[padded, :]
        corr_out[here, :] = change * 2.0
        d_out[here, :] = jnp.where(last, end1, g * change + end1 - g * a1[padded, :]) * 2.0

    over_chunks(span - 2 * PAD, finish)


def own_start(h, p, rows):
    return aligned(part_start(h, p, rows) + PAD * (h + p))


def stage_kernel(rows, p, chips, gain, d, came, *rest):
    out, passed = rest[-2:]
    tail = rest[0].shape[0] if len(rest) == 3 else 0
    body_rows = d.shape[0] - tail
    h, chip, last = place(chips)
    off = part_start(h, p, rows) if tail else own_start(h, p, rows)
    near, far = chip ^ (1 + p), chip ^ (2 - p)

    def exponent(to, at):
        return to - (at + 1) % chips

    def weight(e, square, fourth):
        value = jnp.where((e & 1) == 1, square, 1.0) * jnp.where(e >= 2, fourth, 1.0)
        return jnp.where(e < 0, 0.0, value)

    def one(here, g):
        square = g * g
        fourth = square * square
        mine, its = d[here, :], came[here, :]
        out[here, :] = (
            weight(exponent(chip, chip), square, fourth) * mine + weight(exponent(chip, near), square, fourth) * its
        )
        passed[here, :] = (
            weight(exponent(far, chip), square, fourth) * mine + weight(exponent(far, near), square, fourth) * its
        )

    over_chunks(body_rows, lambda base, n: one(pl.ds(base, n), gain[pl.ds(aligned(off + base), n), :]))
    if tail:
        one(pl.ds(body_rows, tail), rest[0][...])


def last_kernel(rows, p, chips, sums, came, gain, corr, own, send):
    h, _, _ = place(chips)
    off = own_start(h, p, rows)

    def body(base, n):
        here = pl.ds(base, n)
        new0 = sums[here, :] + came[here, :]
        new1 = gain[pl.ds(aligned(off + base), n), :] * new0 + corr[here, :]
        own[here, :] = jnp.where(h == 0, new0, new1)
        send[here, :] = jnp.where(h == 0, new1, new0)

    over_chunks(sums.shape[0], body)


def put_kernel(half, places, chips, *refs):
    out, sems = refs[-2:]
    h, _, _ = place(chips)
    copies = []
    for i, (other, p) in enumerate(places):
        side = 1 - h if other else h
        to = out.at[pl.ds(aligned(side * half + p * (half // 2)), half // 2), :]
        copies.append(pltpu.make_async_copy(refs[i], to, sems.at[i]))
        copies[-1].start()
    for copy in copies:
        copy.wait()


def put(half, places, chips, parts, into=None):
    anywhere = pl.BlockSpec(memory_space=pl.ANY)
    count = len(parts)
    return pl.pallas_call(
        functools.partial(put_kernel, half, places, chips),
        out_shape=jax.ShapeDtypeStruct((2 * half, parts[0].shape[1]), jnp.float32),
        in_specs=[VMEM] * count + ([anywhere] if into is not None else []),
        out_specs=anywhere,
        scratch_shapes=[pltpu.SemaphoreType.DMA((count,))],
        input_output_aliases={count: 0} if into is not None else {},
        compiler_params=PARAMS,
        cost_estimate=pl.CostEstimate(flops=0, bytes_accessed=count * parts[0].size * 8, transcendentals=0),
    )(*parts, *(() if into is None else (into,)))


def call(kernel, outs, scratch=(), cost=None):
    def run(*operands):
        return pl.pallas_call(
            kernel,
            out_shape=[jax.ShapeDtypeStruct(shape, jnp.float32) for shape in outs],
            in_specs=[VMEM] * len(operands),
            out_specs=[VMEM] * len(outs),
            scratch_shapes=[pltpu.VMEM(shape, jnp.float32) for shape in scratch],
            compiler_params=PARAMS,
            cost_estimate=cost,
        )(*operands)

    return run


def scan_plan(chips):
    levels = chips.bit_length() - 1
    every = range(chips)
    end = chips - 1
    own = [end if c == end else -1 for c in every]
    rising = []
    for b in range(levels):
        size = 1 << b
        into, keep, came = [], [], []
        for c in every:
            closes = (c >> (b + 1)) == (end >> (b + 1))
            if c & size:
                into.append(c % size)
                keep.append(0)
                came.append(-1 if closes else size)
            else:
                into.append(c if closes else -1)
                keep.append(-1 if closes else size)
                came.append(0)
        rising.append((b, into, keep, came))
    if levels != 2:
        return own, (rising, rising)

    def weight(to, at):
        return max(to - (at + 1) % chips, -1)

    both = []
    for one, two in ((1, 2), (2, 1)):
        first = [[weight(c, c ^ one) for c in every], [weight(c ^ two, c) for c in every]]
        first.append([weight(c ^ two, c ^ one) for c in every])
        both.append([(one.bit_length() - 1, *first), (two.bit_length() - 1,)])
    return own, tuple(both)


def power(square, exponents, chip):
    e = jnp.asarray(np.array(exponents, np.int32))[chip]
    value, factor = jnp.ones_like(square), square
    for k in range(max(max(exponents), 0).bit_length()):
        value = jnp.where((e >> k) & 1 == 1, value * factor, value)
        factor = factor * factor
    return jnp.where(e < 0, jnp.float32(0.0), value)


def exchange(value, bit, count):
    return lax.ppermute(value, "tm", [(i, i ^ (2 << bit)) for i in range(count)])


def scan(parts, gain, folds, rows, h, chip, chips, count):
    own, orders = scan_plan(chips)
    if len(orders[0]) == 2:
        arrived = [exchange(d, order[0][0], count) for d, order in zip(parts, orders)]
        arrived = [lax.optimization_barrier((r, parts[1 - p]))[0] for p, r in enumerate(arrived)]
        mid = [
            call(functools.partial(stage_kernel, rows, p, chips), (d.shape, d.shape))(gain, d, r, *fold)
            for p, (d, r, fold) in enumerate(zip(parts, arrived, folds))
        ]
        came = [exchange(passed, order[1][0], count) for (_, passed), order in zip(mid, orders)]
        return [out for out, _ in mid], came
    squares = []
    for p, (d, fold) in enumerate(zip(parts, folds)):
        plain = d.shape[0] - sum(f.shape[0] for f in fold)
        off = PAD * h + p * ((rows - 2 * PAD) // 2 - PAD)
        if not fold:
            off = off + PAD * (h + p)
        g = jnp.concatenate([lax.dynamic_slice(gain, (off, 0), (plain, d.shape[1])), *fold], axis=0)
        squares.append(g * g)
    sums = [power(sq, own, chip) * d for sq, d in zip(squares, parts)]
    passed = list(parts)
    for stage in range(len(orders[0])):
        arrived = [exchange(d, order[stage][0], count) for d, order in zip(passed, orders)]
        for p, order in enumerate(orders):
            _, into, keep, came = order[stage]
            sums[p] = sums[p] + power(squares[p], into, chip) * arrived[p]
            passed[p] = power(squares[p], keep, chip) * passed[p] + power(squares[p], came, chip) * arrived[p]
    return sums, [jnp.zeros_like(x) for x in sums]


def local(initial_starts, source, region, base_reluctivity, saturation, mobility):
    potential, driver = initial_starts[0], source[0]
    radial, lanes = potential.shape
    count = lax.axis_size("tm")
    chips = count // 2
    spaces = lax.axis_size("space")
    slot = lax.axis_index("tm")
    h, chip = slot % 2, slot // 2
    half = radial // 2
    margin = -(-HALO // 8) * 8
    rows, start = half + margin, half - margin
    table = jnp.concatenate([base_reluctivity, saturation, mobility])
    table = jnp.broadcast_to(table[:, None], (table.shape[0], lanes))
    partner = [(i, i ^ 1) for i in range(count)]
    slab, padded = (rows, lanes), (rows + 2 * PAD, lanes)
    span = half // 2 + 2 * PAD
    tail = 8 * fold_tiles(span)
    part, plain, room = (span + tail, lanes), (span, lanes), (span + 2 * PAD, lanes)
    cost = pl.CostEstimate(flops=240 * rows * lanes, bytes_accessed=40 * rows * lanes, transcendentals=0)

    there = (1 - h) * start
    send = jnp.concatenate(
        [lax.dynamic_slice(x, (there, 0), slab) for x in (potential, driver)], axis=0
    )
    got = lax.ppermute(send, "tm", partner)
    a0, a1, j0, j1, kind, to_west, to_east = call(
        functools.partial(pack_kernel, rows, start, chips), (padded, padded, slab, slab, slab, plain, plain), cost=cost
    )(potential, driver, got, region)
    from_east = lax.ppermute(to_west, "space", [((i + 1) % spaces, i) for i in range(spaces)])
    from_west = lax.ppermute(to_east, "space", [(i, (i + 1) % spaces) for i in range(spaces)])
    f0, f1, top, slope, mob, gain, a_own, j_own, id_own = call(
        functools.partial(main_kernel, rows), (padded, padded) + (slab,) * 7, (padded,) * 12, cost=cost
    )(table, kind, a0, a1, j0, j1)

    sums, strips, folds = [], [], []
    for p in range(2):
        d, *strip = call(
            functools.partial(strip_kernel, rows, span, p, chips),
            (part,) + (plain,) * 7, (room,) * 3 + (plain,) + (room,) * 4, cost=cost,
        )(table, from_west, from_east, a_own, j_own, id_own, a0, a1, f0, f1, gain)
        sums.append(d)
        strips.append(strip)
        folds.append(call(functools.partial(fold_kernel, span), ((tail, lanes),))(strip[5]))
    sums, came = scan(sums, gain, folds, rows, h, chip, chips, count)

    quarter = (half // 2, lanes)
    ends, sums_2, corrs = [], [], []
    for p in range(2):
        corr, corr_s, top_s, slope_s, mob_s, gain_s, j_s = strips[p]
        end_own, end_send, d, change = call(
            functools.partial(second_kernel, rows, span, p, chips),
            (quarter,) * 4, (room,) * 9 + (plain, (tail, lanes)) + (room,) * 12, cost=cost,
        )(sums[p], came[p], corr, corr_s, gain, top, slope, mob, j0, j1, gain_s, top_s, slope_s, mob_s, j_s)
        ends += [end_own, lax.ppermute(end_send, "tm", partner)]
        sums_2.append(d)
        corrs.append(change)
    places = ((0, 0), (1, 0), (0, 1), (1, 1))
    sums, came = scan(sums_2, gain, [(), ()], rows, h, chip, chips, count)
    ends = put(half, places, chips, ends)
    starts = None
    for p in range(2):
        change = corrs[p]
        if p == 1:
            change, ends, starts = lax.optimization_barrier((change, ends, starts))
        new_own, new_send = call(functools.partial(last_kernel, rows, p, chips), (quarter, quarter))(
            sums[p], came[p], gain, change
        )
        new_got = lax.ppermute(new_send, "tm", partner)
        starts = put(half, places[2 * p : 2 * p + 2], chips, (new_own, new_got), starts)
    return (starts[None], ends[None])


def solution(mesh):
    placed = (P("tm", None, "space"), P("tm", None, "space"), P(None, "space"), P(), P(), P())
    return jax.shard_map(
        local,
        mesh=mesh,
        in_specs=placed,
        out_specs=(P("tm", None, "space"), P("tm", None, "space")),
        check_vma=False,
    )
```
